256 devices in a mesh: wide: 128 (over z, y, x), narrow: 2 (over core).
Axes of the slice: x: 4, y: 4, z: 8, core: 2. Of those that a mesh axis runs over, the one named last changes fastest.
Arguments:
- queries: bfloat16 [32768, 2048], P(('wide', 'narrow')), may hold values from -6 to 6
- keys: bfloat16 [32768, 2048], P(('wide', 'narrow')), may hold values from -6 to 6
- values: bfloat16 [32768, 2048], P(('wide', 'narrow')), may hold values from -6 to 6
Outputs:
- attended: bfloat16 [32768, 2048], P(('wide', 'narrow'))
The draws below stay inside these ranges and needn't reach their ends.
All inputs are finite; a program needn't handle non-finite values.
Results may differ from the reference program's by a relative error of at most 0.008.
Values sent between devices are 32-bit elements; how exact they have to be, the bound alone decides.
A program may use at most 192 MiB of HBM per device.

```python
import jax
import jax.numpy as jnp
from jax import lax

HEADS = 16
HEAD_DIM = 128
TOK_DEV = 128
SEQ = 32768
WIDTH = 2048


def steps_of(own_key, extent, split, low, top_value):
    gain, own = 1.0, jax.random.fold_in(own_key, 6)
    for dim, parts in split:
        steps = jnp.exp(jax.random.uniform(jax.random.fold_in(own, dim), (parts,), jnp.float32, low / len(split), top_value / len(split)))
        gain = gain * jnp.repeat(steps, extent[dim] // parts).reshape([-1 if axis == dim else 1 for axis in range(len(extent))])
    return gain


def scatter_about(stream_key, shape, scale, reach, split=(), kind=jnp.bfloat16):
    result = jax.random.normal(stream_key, shape, jnp.float32) * scale
    if len(split) > 0:
        result = steps_of(stream_key, shape, split, -0.22, 0.18) * result
    return jnp.clip(result, min=-reach, max=reach).astype(kind)


def setup_inputs(seed: int = 0) -> dict:
    key_list = jax.random.split(jax.random.key(seed), 4)
    queries = scatter_about(key_list[0], (SEQ, WIDTH), 1.0, 6.0, ((0, 256),))
    keys = scatter_about(key_list[1], (SEQ, WIDTH), 1.0, 6.0, ((0, 256),))
    values = scatter_about(key_list[2], (SEQ, WIDTH), 1.0, 6.0, ((0, 256),))
    return dict(queries=queries, keys=keys, values=values)


def reference(queries, keys, values):
    blocks = SEQ // TOK_DEV
    qs = queries.reshape(blocks, TOK_DEV, HEADS, HEAD_DIM)
    ks = keys.reshape(blocks, TOK_DEV, HEADS, HEAD_DIM)
    vs = values.reshape(blocks, TOK_DEV, HEADS, HEAD_DIM)
    rows = jnp.arange(TOK_DEV, dtype=jnp.int32)
    causal = rows[None, :, None] >= rows[None, None, :]

    def step(state, block):
        q_blk, k_blk, v_blk = block
        qf = q_blk.astype(jnp.float32)
        kf = k_blk.astype(jnp.float32)
        vf = v_blk.astype(jnp.float32)
        scores = jnp.einsum('thd,shd->hts', qf, kf)
        scores = jnp.where(causal, scores, 0.0).astype(jnp.bfloat16)
        local = jnp.einsum('hts,shd->thd', scores.astype(jnp.float32), vf)
        carried = jnp.einsum('thd,hde->the', qf, state, precision=lax.Precision.HIGHEST)
        total = local + carried
        scale = lax.rsqrt(lax.optimization_barrier(jnp.mean(total * total, axis=-1, keepdims=True)) + 1e-05)
        out = (total * scale).astype(jnp.bfloat16)
        new_state = state + jnp.einsum('shd,she->hde', kf, vf)
        return (new_state, out)
    start = jnp.zeros((HEADS, HEAD_DIM, HEAD_DIM), jnp.float32)
    _, outs = lax.scan(step, start, (qs, ks, vs))
    return outs.reshape(SEQ, HEADS * HEAD_DIM)
```

```python
import functools

import jax
import jax.numpy as jnp
from jax import lax
from jax.experimental import pallas as pl
from jax.experimental.pallas import tpu as pltpu
from jax.sharding import PartitionSpec as P

HEADS = 16
DIM = 128
GROUP = HEADS // 2
CHUNKS = 4
PER = GROUP // CHUNKS
ROWS = PER * DIM
NX, NY, NZ = 4, 4, 8
PLANE = NX * NY
SLICE = ROWS // PLANE
MESH = pl.DeviceIdType.MESH


def dot(a, b, dims):
    return lax.dot_general(a, b, (dims, ((), ())), preferred_element_type=jnp.float32)


def kernel(q_ref, k_ref, v_ref, o_ref, own, part, total, up, prefix, plane, zrecv, down, carry, give, other, local,
           ex_send, ex_recv, up_send, up_recv, z_send, z_recv, dn_send, dn_recv, fx_send, fx_recv):
    wide, core = lax.axis_index("wide"), lax.axis_index("narrow")
    here = wide % PLANE
    z = wide // PLANE
    partner = (wide, 1 - core)

    def chip_in_plane(i):
        return z * PLANE + i

    def remote(src, dst, send, recv, to):
        return pltpu.make_async_remote_copy(src, dst, send, recv, device_id=to, device_id_type=MESH)

    def arrived(ref, sem):
        pltpu.make_async_copy(ref, ref, sem).wait()

    barrier = pltpu.get_barrier_semaphore()
    pl.semaphore_signal(barrier, inc=1, device_id=partner, device_id_type=MESH)
    for i in range(1, PLANE):
        pl.semaphore_signal(barrier, inc=1, device_id=(chip_in_plane((here + i) % PLANE), core), device_id_type=MESH)
    for i in range(1, NZ):
        pl.semaphore_signal(barrier, inc=1, device_id=(((z + i) % NZ) * PLANE + here, core), device_id_type=MESH)

    def columns(group, head):
        return pl.ds(pl.multiple_of(group * (GROUP * DIM) + head * DIM, DIM), DIM)

    def states(group):
        for head in range(GROUP):
            at = columns(group, head)
            own[group, head // PER, pl.ds((head % PER) * DIM, DIM), :] = dot(k_ref[:, at], v_ref[:, at], ((0,), (0,)))

    states(1 - core)
    pl.semaphore_wait(barrier, PLANE - 1 + NZ - 1 + 1)
    for k in range(CHUNKS):
        remote(own.at[1 - core, k], part.at[k], ex_send.at[k], ex_recv.at[k], partner).start()
    states(core)

    for k in range(CHUNKS):
        arrived(part.at[k], ex_recv.at[k])
        summed = own[core, k] + part[k]
        total[k] = summed.reshape(PLANE, SLICE, DIM)
        up[k, here] = total[k, here]
        for i in range(1, PLANE):
            root = (here + i) % PLANE
            remote(total.at[k, root], up.at[k, here], up_send.at[k], up_recv.at[k], (chip_in_plane(root), core)).start()

    rows = lax.broadcasted_iota(jnp.int32, (DIM, DIM), 0)
    cols = lax.broadcasted_iota(jnp.int32, (DIM, DIM), 1)
    causal = rows >= cols
    for head in range(HEADS):
        at = pl.ds(head * DIM, DIM)
        scores = dot(q_ref[:, at], k_ref[:, at], ((1,), (1,)))
        scores = jnp.where(causal, scores, 0.0).astype(jnp.bfloat16)
        local[:, at] = dot(scores, v_ref[:, at], ((1,), (0,)))

    for k in range(CHUNKS):
        arrived(up.at[k, pl.ds(0, PLANE - 1)], up_recv.at[k])
        before = jnp.zeros((SLICE, DIM), jnp.float32)
        for i in range(PLANE):
            prefix[k, i] = before
            before = before + up[k, i]
        plane[k] = before

        @pl.loop(z + 1, NZ)
        def _(to):
            remote(plane.at[k], zrecv.at[k, z], z_send.at[k, to], z_recv.at[k, z], (to * PLANE + here, core)).start()

    for k in range(CHUNKS):
        def add(frm, acc):
            arrived(zrecv.at[k, frm], z_recv.at[k, frm])
            return acc + zrecv[k, frm]

        below = lax.fori_loop(0, z, add, jnp.zeros((SLICE, DIM), jnp.float32))
        down[k] = prefix[k] + below[None]
        carry[k, here] = down[k, here]
        for i in range(1, PLANE):
            chip = (here + i) % PLANE
            remote(down.at[k, chip], carry.at[k, here], dn_send.at[k], dn_recv.at[k], (chip_in_plane(chip), core)).start()

    def finish(group, head, state):
        at = columns(group, head)
        high = state.astype(jnp.bfloat16)
        low = (state - high.astype(jnp.float32)).astype(jnp.bfloat16)
        q = q_ref[:, at]
        whole = local[:, at] + (dot(q, high, ((1,), (0,))) + dot(q, low, ((1,), (0,))))
        factor = lax.rsqrt(jnp.mean(whole * whole, axis=-1, keepdims=True) + 1e-05)
        o_ref[:, at] = (whole * factor).astype(jnp.bfloat16)

    for k in range(CHUNKS):
        arrived(carry.at[k, pl.ds(0, PLANE - 1)], dn_recv.at[k])
        chip_carry = carry[k].reshape(ROWS, DIM)
        give[k] = chip_carry + jnp.where(core == 0, own[core, k], 0.0)
        remote(give.at[k], other.at[k], fx_send.at[k], fx_recv.at[k], partner).start()
        mine = chip_carry + jnp.where(core == 0, 0.0, part[k])
        for j in range(PER):
            finish(core, k * PER + j, mine[j * DIM:(j + 1) * DIM])

    for k in range(CHUNKS):
        arrived(other.at[k], fx_recv.at[k])
        for j in range(PER):
            finish(1 - core, k * PER + j, other[k, pl.ds(j * DIM, DIM), :])

    for k in range(CHUNKS):
        arrived(own.at[1 - core, k], ex_send.at[k])
        arrived(total.at[k, pl.ds(0, PLANE - 1)], up_send.at[k])
        arrived(down.at[k, pl.ds(0, PLANE - 1)], dn_send.at[k])
        arrived(give.at[k], fx_send.at[k])

        @pl.loop(z + 1, NZ)
        def _(to):
            arrived(plane.at[k], z_send.at[k, to])


def shards(queries, keys, values):
    f32 = jnp.float32
    dma = pltpu.SemaphoreType.DMA
    vmem = pl.BlockSpec(memory_space=pltpu.VMEM)
    return pl.pallas_call(
        kernel,
        out_shape=jax.ShapeDtypeStruct(queries.shape, queries.dtype),
        in_specs=[vmem] * 3,
        out_specs=vmem,
        scratch_shapes=[
            pltpu.VMEM((2, CHUNKS, ROWS, DIM), f32),
            pltpu.VMEM((CHUNKS, ROWS, DIM), f32),
            pltpu.VMEM((CHUNKS, PLANE, SLICE, DIM), f32),
            pltpu.VMEM((CHUNKS, PLANE, SLICE, DIM), f32),
            pltpu.VMEM((CHUNKS, PLANE, SLICE, DIM), f32),
            pltpu.VMEM((CHUNKS, SLICE, DIM), f32),
            pltpu.VMEM((CHUNKS, NZ, SLICE, DIM), f32),
            pltpu.VMEM((CHUNKS, PLANE, SLICE, DIM), f32),
            pltpu.VMEM((CHUNKS, PLANE, SLICE, DIM), f32),
            pltpu.VMEM((CHUNKS, ROWS, DIM), f32),
            pltpu.VMEM((CHUNKS, ROWS, DIM), f32),
            pltpu.VMEM((DIM, HEADS * DIM), f32),
            dma((CHUNKS,)), dma((CHUNKS,)), dma((CHUNKS,)), dma((CHUNKS,)),
            dma((CHUNKS, NZ)), dma((CHUNKS, NZ)),
            dma((CHUNKS,)), dma((CHUNKS,)), dma((CHUNKS,)), dma((CHUNKS,)),
        ],
        compiler_params=pltpu.CompilerParams(collective_id=0, has_side_effects=True),
        name="prefix_attention",
    )(queries, keys, values)


def solution(mesh):
    placed = P(("wide", "narrow"), None)
    return jax.shard_map(shards, mesh=mesh, in_specs=(placed,) * 3, out_specs=placed, check_vma=False)
```

```python
import contextlib

import jax
import jax.numpy as jnp
from jax import lax
from jax.experimental import pallas as pl
from jax.experimental.pallas import tpu as pltpu
from jax.sharding import PartitionSpec as P

HEADS = 16
DIM = 128
GROUP = HEADS // 2
CHUNKS = ((0, 2), (2, 2), (4, 2), (6, 1), (7, 1))
N = len(CHUNKS)
NZ = 8
HALF = NZ // 2
PLANE = 16
PIECE = DIM // PLANE
LAGS = (0, 1, 1, 1, 1, 1, 2, 2)
MESH = pl.DeviceIdType.MESH


def scope(name):
    return contextlib.nullcontext()


def dot(a, b, dims):
    return lax.dot_general(a, b, (dims, ((), ())), preferred_element_type=jnp.float32)


def kernel(q_hbm, k_hbm, v_hbm, o_ref, q_ref, k_ref, v_ref, own, part, total, up, prefix, plane, below, zrecv, down,
           carry, give, other, local, in_sem, hello, go,
           ex_send, ex_recv, up_send, up_recv, z_send, z_recv, dn_send, dn_recv, fx_send, fx_recv):
    wide, core = lax.axis_index("wide"), lax.axis_index("narrow")
    here = wide % PLANE
    z = wide // PLANE
    partner = (wide, 1 - core)
    z_first = jnp.where(z < HALF, 0, HALF - 1)
    z_last = jnp.where(z < HALF, HALF, NZ)

    def chip_in_plane(i):
        return z * PLANE + i

    def remote(src, dst, send, recv, to):
        return pltpu.make_async_remote_copy(src, dst, send, recv, device_id=to, device_id_type=MESH)

    def arrived(ref, sem):
        pltpu.make_async_copy(ref, ref, sem).wait()

    def rows(k):
        first, count = CHUNKS[k]
        return pl.ds(first * DIM, count * DIM)

    def slice_of(k, i):
        first, count = CHUNKS[k]
        return pl.ds(pl.multiple_of(first * DIM + i * (count * PIECE), 8), count * PIECE)

    def root_rows(k):
        first, count = CHUNKS[k]
        return pl.ds(first * PIECE, count * PIECE)

    def all_but_one(k):
        first, count = CHUNKS[k]
        return pl.ds(first * DIM, (PLANE - 1) * count * PIECE)

    with scope("a_sig"):
        barrier = pltpu.get_barrier_semaphore()

        @pl.when(core == 0)
        def _():
            pl.semaphore_signal(barrier, inc=1, device_id=partner, device_id_type=MESH)

        for i in range(1, PLANE):
            pl.semaphore_signal(barrier, inc=1, device_id=(chip_in_plane((here + i) % PLANE), 0), device_id_type=MESH)

        @pl.loop(z_first, z)
        def _(frm):
            pl.semaphore_signal(barrier, inc=1, device_id=(frm * PLANE + here, 0), device_id_type=MESH)

        loads = [pltpu.make_async_copy(src, dst, in_sem.at[i])
                 for i, (src, dst) in enumerate(((k_hbm, k_ref), (v_hbm, v_ref), (q_hbm, q_ref)))]
        for load in loads:
            load.start()

        @pl.when(core == 1)
        def _():
            pl.semaphore_wait(barrier, 1)
            pl.semaphore_signal(hello, inc=1, device_id=partner, device_id_type=MESH)

        @pl.when(core == 0)
        def _():
            pl.semaphore_wait(hello, 1)

    def columns(group, head, count=1):
        return pl.ds(pl.multiple_of(group * (GROUP * DIM) + head * DIM, DIM), count * DIM)

    def states(group, k):
        first, count = CHUNKS[k]
        for head in range(first, first + count):
            at = columns(group, head)
            own[group, pl.ds(head * DIM, DIM), :] = dot(k_ref[:, at], v_ref[:, at], ((0,), (0,)))

    with scope("b_load"):
        loads[0].wait()
        loads[1].wait()
    with scope("b_states"):
        for k in range(N):
            states(1 - core, k)
            remote(own.at[1 - core, rows(k)], part.at[rows(k)], ex_send.at[k], ex_recv.at[k], partner).start()
        for k in range(N):
            states(core, k)
    with scope("c_barrier"):
        @pl.when(core == 0)
        def _():
            z_peers = jnp.where(z == HALF - 1, HALF, z_last - 1 - z)
            pl.semaphore_wait(barrier, 2 * (PLANE - 1 + z_peers))
            pl.semaphore_signal(go, inc=1, device_id=partner, device_id_type=MESH)

        @pl.when(core == 1)
        def _():
            pl.semaphore_wait(go, 1)

    for k in range(N):
        with scope(f"f_exwait{k}"):
            arrived(part.at[rows(k)], ex_recv.at[k])
        with scope(f"f_up{k}"):
            total[rows(k)] = own[core, rows(k)] + part[rows(k)]
            up[slice_of(k, here)] = total[slice_of(k, here)]
            for i in range(1, PLANE):
                root = (here + i) % PLANE
                remote(total.at[slice_of(k, root)], up.at[slice_of(k, here)], up_send.at[k], up_recv.at[k],
                       (chip_in_plane(root), core)).start()

    with scope("g_local"):
        loads[2].wait()
        causal = lax.broadcasted_iota(jnp.int32, (DIM, DIM), 0) >= lax.broadcasted_iota(jnp.int32, (DIM, DIM), 1)
        for head in range(HEADS):
            at = pl.ds(head * DIM, DIM)
            scores = dot(q_ref[:, at], k_ref[:, at], ((1,), (1,)))
            scores = jnp.where(causal, scores, 0.0).astype(jnp.bfloat16)
            local[:, at] = dot(scores, v_ref[:, at], ((1,), (0,)))

    def to_plane(source, k, to):
        return remote(source.at[root_rows(k)], zrecv.at[z, root_rows(k)], z_send.at[k, to], z_recv.at[k, z],
                      (to * PLANE + here, core))

    def root(k):
        with scope(f"h_upwait{k}"):
            arrived(up.at[all_but_one(k)], up_recv.at[k])
        with scope(f"h_root{k}"):
            before = jnp.zeros((CHUNKS[k][1] * PIECE, DIM), jnp.float32)
            for i in range(PLANE):
                prefix[slice_of(k, i)] = before
                before = before + up[slice_of(k, i)]
            plane[root_rows(k)] = before

            @pl.loop(z + 1, z_last)
            def _(to):
                to_plane(plane, k, to).start()

    def carries(k):
        def add(frm, acc):
            arrived(zrecv.at[frm, root_rows(k)], z_recv.at[k, frm])
            return acc + zrecv[frm, root_rows(k)]

        with scope(f"i_zwait{k}"):
            earlier = lax.fori_loop(z_first, z, add, jnp.zeros((CHUNKS[k][1] * PIECE, DIM), jnp.float32))

        with scope(f"i_down{k}"):
            @pl.when(z == HALF - 1)
            def _():
                below[root_rows(k)] = earlier + plane[root_rows(k)]
                for to in range(HALF, NZ):
                    to_plane(below, k, to).start()

            for i in range(PLANE):
                down[slice_of(k, i)] = prefix[slice_of(k, i)] + earlier
            carry[slice_of(k, here)] = down[slice_of(k, here)]
            for i in range(1, PLANE):
                chip = (here + i) % PLANE
                remote(down.at[slice_of(k, chip)], carry.at[slice_of(k, here)], dn_send.at[k], dn_recv.at[k],
                       (chip_in_plane(chip), core)).start()

    for step in range(N + max(LAGS)):
        if step < N:
            root(step)
        for lag in sorted(set(LAGS)):
            if 0 <= step - lag < N:
                wanted = [i for i in range(NZ) if LAGS[i] == lag]

                @pl.when((z >= wanted[0]) & (z <= wanted[-1]))
                def _():
                    carries(step - lag)

    def finish(group, head, state):
        at = columns(group, head)
        high = state.astype(jnp.bfloat16)
        low = (state - high.astype(jnp.float32)).astype(jnp.bfloat16)
        q = q_ref[:, at]
        whole = local[:, at] + (dot(q, high, ((1,), (0,))) + dot(q, low, ((1,), (0,))))
        factor = lax.rsqrt(jnp.mean(whole * whole, axis=-1, keepdims=True) + 1e-05)
        o_ref[:, at] = (whole * factor).astype(jnp.bfloat16)

    def finish_other(k):
        with scope(f"k_fxwait{k}"):
            arrived(other.at[rows(k)], fx_recv.at[k])
        with scope(f"k_fin{k}"):
            first, count = CHUNKS[k]
            for head in range(first, first + count):
                finish(1 - core, head, other[pl.ds(head * DIM, DIM)])

    for k in range(N):
        with scope(f"j_dnwait{k}"):
            arrived(carry.at[all_but_one(k)], dn_recv.at[k])
        with scope(f"j_fin{k}"):
            give[rows(k)] = carry[rows(k)] + jnp.where(core == 0, own[core, rows(k)], 0.0)
            remote(give.at[rows(k)], other.at[rows(k)], fx_send.at[k], fx_recv.at[k], partner).start()
            first, count = CHUNKS[k]
            for head in range(first, first + count):
                at = pl.ds(head * DIM, DIM)
                finish(core, head, carry[at] + jnp.where(core == 0, 0.0, part[at]))
        if k:
            finish_other(k - 1)
    finish_other(N - 1)

    with scope("l_waits"):
        for k in range(N):
            arrived(own.at[1 - core, rows(k)], ex_send.at[k])
            arrived(total.at[all_but_one(k)], up_send.at[k])
            arrived(down.at[all_but_one(k)], dn_send.at[k])
            arrived(give.at[rows(k)], fx_send.at[k])

            @pl.loop(z + 1, z_last)
            def _(to):
                arrived(plane.at[root_rows(k)], z_send.at[k, to])

            @pl.when(z == HALF - 1)
            def _():
                for to in range(HALF, NZ):
                    arrived(below.at[root_rows(k)], z_send.at[k, to])


def shards(queries, keys, values):
    dma = pltpu.SemaphoreType.DMA
    hbm = pl.BlockSpec(memory_space=pltpu.HBM)
    block = pltpu.VMEM(queries.shape, queries.dtype)
    state = pltpu.VMEM((GROUP * DIM, DIM), jnp.float32)
    root = pltpu.VMEM((GROUP * PIECE, DIM), jnp.float32)
    return pl.pallas_call(
        kernel,
        out_shape=pltpu.VMEM(queries.shape, queries.dtype),
        in_specs=[hbm] * 3,
        out_specs=pl.BlockSpec(memory_space=pltpu.VMEM),
        scratch_shapes=[
            block, block, block,
            pltpu.VMEM((2, GROUP * DIM, DIM), jnp.float32),
            state, state, state, state, root, root,
            pltpu.VMEM((NZ, GROUP * PIECE, DIM), jnp.float32),
            state, state, state, state,
            pltpu.VMEM((DIM, HEADS * DIM), jnp.float32),
            dma((3,)), pltpu.SemaphoreType.REGULAR, pltpu.SemaphoreType.REGULAR,
            dma((N,)), dma((N,)), dma((N,)), dma((N,)),
            dma((N, NZ)), dma((N, NZ)),
            dma((N,)), dma((N,)), dma((N,)), dma((N,)),
        ],
        compiler_params=pltpu.CompilerParams(collective_id=0, has_side_effects=True),
        name="prefix_attention",
    )(*(pltpu.with_memory_space_constraint(x, pltpu.HBM) for x in (queries, keys, values)))


def solution(mesh):
    placed = P(("wide", "narrow"), None)
    return jax.shard_map(shards, mesh=mesh, in_specs=(placed,) * 3, out_specs=placed, check_vma=False)
```

```python
import contextlib
import functools

import jax
import jax.numpy as jnp
from jax import lax
from jax.experimental import pallas as pl
from jax.experimental.pallas import tpu as pltpu
from jax.sharding import PartitionSpec as P

HEADS = 16
DIM = 128
GROUP = HEADS // 2
CHUNKS = ((0, 2), (2, 2), (4, 2), (6, 1), (7, 1))
N = len(CHUNKS)
NZ = 8
HALF = NZ // 2
PLANE = 16
PIECE = DIM // PLANE
LAGS = (0, 1, 1, 2, 3, 3, 3, 3)
MESH = pl.DeviceIdType.MESH


def scope(name):
    return contextlib.nullcontext()


def dot(a, b, dims):
    return lax.dot_general(a, b, (dims, ((), ())), preferred_element_type=jnp.float32)


def kernel(q_hbm, k_hbm, v_hbm, o_ref, q_ref, k_ref, v_ref, own, part, total, up, prefix, plane, below, pair, zrecv, down,
           carry, give, other, local, in_sem, hello, go,
           ex_send, ex_recv, up_send, up_recv, z_send, z_recv, dn_send, dn_recv, fx_send, fx_recv):
    wide, core = lax.axis_index("wide"), lax.axis_index("narrow")
    here = wide % PLANE
    z = wide // PLANE
    partner = (wide, 1 - core)
    z_first = jnp.where(z < HALF, 0, 1)
    z_last = jnp.where(z < 2, HALF, NZ)

    def chip_in_plane(i):
        return z * PLANE + i

    def remote(src, dst, send, recv, to):
        return pltpu.make_async_remote_copy(src, dst, send, recv, device_id=to, device_id_type=MESH)

    def arrived(ref, sem):
        pltpu.make_async_copy(ref, ref, sem).wait()

    def rows(k):
        first, count = CHUNKS[k]
        return pl.ds(first * DIM, count * DIM)

    def slice_of(k, i):
        first, count = CHUNKS[k]
        return pl.ds(pl.multiple_of(first * DIM + i * (count * PIECE), 8), count * PIECE)

    def root_rows(k):
        first, count = CHUNKS[k]
        return pl.ds(first * PIECE, count * PIECE)

    def all_but_one(k):
        first, count = CHUNKS[k]
        return pl.ds(first * DIM, (PLANE - 1) * count * PIECE)

    with scope("a_sig"):
        barrier = pltpu.get_barrier_semaphore()
        late = (z < HALF) | ((z < NZ - 1) & (here % 4 >= 2) & (here >= PLANE // 2))

        @pl.when(jnp.where(late, 1, 0) == core)
        def _():
            pl.semaphore_signal(barrier, inc=1, device_id=partner, device_id_type=MESH)

        for i in range(1, PLANE):
            pl.semaphore_signal(barrier, inc=1, device_id=(chip_in_plane((here + i) % PLANE), 0), device_id_type=MESH)

        @pl.loop(z_first, z)
        def _(frm):
            pl.semaphore_signal(barrier, inc=1, device_id=(frm * PLANE + here, 1), device_id_type=MESH)

        loads = [pltpu.make_async_copy(src, dst, in_sem.at[i])
                 for i, (src, dst) in enumerate(((k_hbm, k_ref), (v_hbm, v_ref), (q_hbm, q_ref)))]
        for load in loads:
            load.start()

    z_peers = 2 * (z_last - 1 - z + jnp.where(z == 1, NZ - HALF, 0))

    def meet_above(count):
        @pl.when(core == 1)
        def _():
            pl.semaphore_wait(barrier, count)
            pl.semaphore_signal(hello, inc=1, device_id=partner, device_id_type=MESH)

        @pl.when(core == 0)
        def _():
            pl.semaphore_wait(hello, 1)

    def meet_plane(count):
        @pl.when(core == 0)
        def _():
            pl.semaphore_wait(barrier, count)
            pl.semaphore_signal(go, inc=1, device_id=partner, device_id_type=MESH)

        @pl.when(core == 1)
        def _():
            pl.semaphore_wait(go, 1)

    def exchange():
        for k in range(N):
            remote(own.at[1 - core, rows(k)], part.at[rows(k)], ex_send, ex_recv.at[min(k, 1)], partner).start()

    def columns(group, head, count=1):
        return pl.ds(pl.multiple_of(group * (GROUP * DIM) + head * DIM, DIM), count * DIM)

    def states(group, k):
        first, count = CHUNKS[k]
        for head in range(first, first + count):
            at = columns(group, head)
            own[group, pl.ds(head * DIM, DIM), :] = dot(k_ref[:, at], v_ref[:, at], ((0,), (0,)))

    with scope("b_load"):
        loads[0].wait()
        loads[1].wait()
    with scope("b_states"):
        for k in range(N):
            states(1 - core, k)
            states(core, k)
    with scope("c_barrier"):
        @pl.when(jnp.logical_not(late))
        def _():
            meet_above(z_peers + 1)
            exchange()
            meet_plane(2 * (PLANE - 1))

        @pl.when(late)
        def _():
            meet_plane(2 * (PLANE - 1) + 1)
            exchange()

    for k in range(N):
        with scope(f"f_exwait{k}"):
            if k < 2:
                rest = GROUP - CHUNKS[k][0] if k else CHUNKS[0][1]
                arrived(part.at[pl.ds(CHUNKS[k][0] * DIM, rest * DIM)], ex_recv.at[k])
        with scope(f"f_up{k}"):
            total[rows(k)] = own[core, rows(k)] + part[rows(k)]
            up[slice_of(k, here)] = total[slice_of(k, here)]
            for i in range(1, PLANE):
                root = (here + i) % PLANE
                remote(total.at[slice_of(k, root)], up.at[slice_of(k, here)], up_send, up_recv.at[k],
                       (chip_in_plane(root), core)).start()

    with scope("g_local"):
        loads[2].wait()
        causal = lax.broadcasted_iota(jnp.int32, (DIM, DIM), 0) >= lax.broadcasted_iota(jnp.int32, (DIM, DIM), 1)
        for head in range(HEADS):
            at = pl.ds(head * DIM, DIM)
            scores = dot(q_ref[:, at], k_ref[:, at], ((1,), (1,)))
            scores = jnp.where(causal, scores, 0.0).astype(jnp.bfloat16)
            local[:, at] = dot(scores, v_ref[:, at], ((1,), (0,)))

    with scope("g_meet"):
        @pl.when(late)
        def _():
            meet_above(z_peers)

    def to_plane(source, k, to):
        return remote(source.at[root_rows(k)], zrecv.at[z, root_rows(k)], z_send, z_recv.at[k],
                      (to * PLANE + here, core))

    def root(k):
        with scope(f"h_upwait{k}"):
            arrived(up.at[all_but_one(k)], up_recv.at[k])
        with scope(f"h_root{k}"):
            before = jnp.zeros((CHUNKS[k][1] * PIECE, DIM), jnp.float32)
            for i in range(PLANE):
                prefix[slice_of(k, i)] = before
                before = before + up[slice_of(k, i)]
            plane[root_rows(k)] = before

            @pl.loop(z + 1, z_last)
            def _(to):
                to_plane(plane, k, to).start()

    def planes_arrived(count, at, sem):
        for n in range(1, NZ - 1):
            @pl.when(count == n)
            def _():
                arrived(zrecv.at[pl.ds(0, n), at], sem)

    def earlier(k):
        with scope(f"i_zwait{k}"):
            planes_arrived(z - z_first, root_rows(k), z_recv.at[k])
            below[root_rows(k)] = lax.fori_loop(z_first, z, lambda frm, acc: acc + zrecv[frm, root_rows(k)],
                                                jnp.zeros((CHUNKS[k][1] * PIECE, DIM), jnp.float32))

        @pl.when(z == 1)
        def _():
            pair[root_rows(k)] = below[root_rows(k)] + plane[root_rows(k)]
            for to in range(HALF, NZ):
                to_plane(pair, k, to).start()

    def carries(k):
        with scope(f"i_down{k}"):
            above = below[root_rows(k)]
            for i in range(PLANE):
                down[slice_of(k, i)] = prefix[slice_of(k, i)] + above
            carry[slice_of(k, here)] = down[slice_of(k, here)]
            for i in range(1, PLANE):
                chip = (here + i) % PLANE
                remote(down.at[slice_of(k, chip)], carry.at[slice_of(k, here)], dn_send, dn_recv.at[k],
                       (chip_in_plane(chip), core)).start()

    for step in range(N + max(LAGS)):
        if step < N:
            root(step)
        for lag in sorted(set(LAGS)):
            if 0 <= step - lag < N:
                wanted = [i for i in range(NZ) if LAGS[i] == lag]

                @pl.when(functools.reduce(jnp.logical_or, [z == i for i in wanted]))
                def _():
                    earlier(step - lag)
                    carries(step - lag)

    def finish(group, head, state):
        at = columns(group, head)
        high = state.astype(jnp.bfloat16)
        low = (state - high.astype(jnp.float32)).astype(jnp.bfloat16)
        q = q_ref[:, at]
        whole = local[:, at] + (dot(q, high, ((1,), (0,))) + dot(q, low, ((1,), (0,))))
        factor = lax.rsqrt(jnp.mean(whole * whole, axis=-1, keepdims=True) + 1e-05)
        o_ref[:, at] = (whole * factor).astype(jnp.bfloat16)

    def finish_other(k):
        with scope(f"k_fxwait{k}"):
            arrived(other.at[rows(k)], fx_recv.at[k])
        with scope(f"k_fin{k}"):
            first, count = CHUNKS[k]
            for head in range(first, first + count):
                finish(1 - core, head, other[pl.ds(head * DIM, DIM)])

    for k in range(N):
        with scope(f"j_dnwait{k}"):
            arrived(carry.at[all_but_one(k)], dn_recv.at[k])
        with scope(f"j_fin{k}"):
            give[rows(k)] = carry[rows(k)] + jnp.where(core == 0, own[core, rows(k)], 0.0)
            remote(give.at[rows(k)], other.at[rows(k)], fx_send, fx_recv.at[k], partner).start()
            first, count = CHUNKS[k]
            for head in range(first, first + count):
                at = pl.ds(head * DIM, DIM)
                finish(core, head, carry[at] + jnp.where(core == 0, 0.0, part[at]))
        if k:
            finish_other(k - 1)
    finish_other(N - 1)

    with scope("l_waits"):
        arrived(own.at[1 - core], ex_send)
        arrived(total.at[pl.ds(0, (PLANE - 1) * GROUP * PIECE)], up_send)
        arrived(down.at[pl.ds(0, (PLANE - 1) * GROUP * PIECE)], dn_send)
        arrived(give, fx_send)
        planes_arrived(z_last - 1 - z + jnp.where(z == 1, NZ - HALF, 0), pl.ds(0, GROUP * PIECE), z_send)


def shards(queries, keys, values):
    dma = pltpu.SemaphoreType.DMA
    hbm = pl.BlockSpec(memory_space=pltpu.HBM)
    block = pltpu.VMEM(queries.shape, queries.dtype)
    state = pltpu.VMEM((GROUP * DIM, DIM), jnp.float32)
    root = pltpu.VMEM((GROUP * PIECE, DIM), jnp.float32)
    return pl.pallas_call(
        kernel,
        out_shape=pltpu.VMEM(queries.shape, queries.dtype),
        in_specs=[hbm] * 3,
        out_specs=pl.BlockSpec(memory_space=pltpu.VMEM),
        scratch_shapes=[
            block, block, block,
            pltpu.VMEM((2, GROUP * DIM, DIM), jnp.float32),
            state, state, state, state, root, root, root,
            pltpu.VMEM((NZ, GROUP * PIECE, DIM), jnp.float32),
            state, state, state, state,
            pltpu.VMEM((DIM, HEADS * DIM), jnp.float32),
            dma((3,)), pltpu.SemaphoreType.REGULAR, pltpu.SemaphoreType.REGULAR,
            dma, dma((2,)), dma, dma((N,)), dma, dma((N,)), dma, dma((N,)), dma, dma((N,)),
        ],
        compiler_params=pltpu.CompilerParams(collective_id=0, has_side_effects=True),
        name="prefix_attention",
    )(*(pltpu.with_memory_space_constraint(x, pltpu.HBM) for x in (queries, keys, values)))


def solution(mesh):
    placed = P(("wide", "narrow"), None)
    return jax.shard_map(shards, mesh=mesh, in_specs=(placed,) * 3, out_specs=placed, check_vma=False)
```

```python
import contextlib
import functools

import jax
import jax.numpy as jnp
from jax import lax
from jax.experimental import pallas as pl
from jax.experimental.pallas import tpu as pltpu
from jax.sharding import PartitionSpec as P

HEADS = 16
DIM = 128
GROUP = HEADS // 2
CHUNKS = ((0, 2), (2, 2), (4, 2), (6, 1), (7, 1))
N = len(CHUNKS)
NZ = 8
HALF = NZ // 2
PLANE = 16
PIECE = DIM // PLANE
LAGS = (0, 1, 1, 2, 2, 2, 2, 2)
SIDE = 4
STEPS = sorted(((dx, dy) for dy in range(SIDE) for dx in range(SIDE) if dx or dy),
               key=lambda step: -sum(min(d, SIDE - d) for d in step))
MESH = pl.DeviceIdType.MESH


def scope(name):
    return contextlib.nullcontext()


def dot(a, b, dims):
    return lax.dot_general(a, b, (dims, ((), ())), preferred_element_type=jnp.float32)


def kernel(q_hbm, k_hbm, v_hbm, o_ref, q_ref, k_ref, v_ref, own, part, total, up, prefix, plane, below, pair, zrecv, down,
           carry, give, other, local, in_sem, hello, go,
           ex_send, ex_recv, up_send, up_recv, z_send, z_recv, dn_send, dn_recv, fx_send, fx_recv):
    wide, core = lax.axis_index("wide"), lax.axis_index("narrow")
    here = wide % PLANE
    z = wide // PLANE
    x, y = here % SIDE, here // SIDE
    others = [(y + dy) % SIDE * SIDE + (x + dx) % SIDE for dx, dy in STEPS]
    partner = (wide, 1 - core)
    z_first = jnp.where(z < HALF, 0, 1)
    z_last = jnp.where(z < 2, HALF, NZ)

    def chip_in_plane(i):
        return z * PLANE + i

    def remote(src, dst, send, recv, to):
        return pltpu.make_async_remote_copy(src, dst, send, recv, device_id=to, device_id_type=MESH)

    def arrived(ref, sem):
        pltpu.make_async_copy(ref, ref, sem).wait()

    def rows(k):
        first, count = CHUNKS[k]
        return pl.ds(first * DIM, count * DIM)

    def slice_of(k, i):
        first, count = CHUNKS[k]
        return pl.ds(pl.multiple_of(first * DIM + i * (count * PIECE), 8), count * PIECE)

    def root_rows(k):
        first, count = CHUNKS[k]
        return pl.ds(first * PIECE, count * PIECE)

    def all_but_one(k):
        first, count = CHUNKS[k]
        return pl.ds(first * DIM, (PLANE - 1) * count * PIECE)

    with scope("a_sig"):
        barrier = pltpu.get_barrier_semaphore()
        late = jnp.where(z == 0, x + y > 1, jnp.where(z == 3, x + y > 2, (z < HALF) | ((z == HALF) & (x >= 2) & (y >= 2))))

        @pl.when(jnp.where(late, 1, 0) == core)
        def _():
            pl.semaphore_signal(barrier, inc=1, device_id=partner, device_id_type=MESH)

        for chip in others:
            pl.semaphore_signal(barrier, inc=1, device_id=(chip_in_plane(chip), 0), device_id_type=MESH)

        @pl.loop(z_first, z)
        def _(frm):
            pl.semaphore_signal(barrier, inc=1, device_id=(frm * PLANE + here, 1), device_id_type=MESH)

        loads = [pltpu.make_async_copy(src, dst, in_sem.at[i])
                 for i, (src, dst) in enumerate(((k_hbm, k_ref), (v_hbm, v_ref), (q_hbm, q_ref)))]
        for load in loads:
            load.start()

    z_peers = 2 * (z_last - 1 - z + jnp.where(z == 1, NZ - HALF, 0))

    def meet_above(count):
        @pl.when(core == 1)
        def _():
            pl.semaphore_wait(barrier, count)
            pl.semaphore_signal(hello, inc=1, device_id=partner, device_id_type=MESH)

        @pl.when(core == 0)
        def _():
            pl.semaphore_wait(hello, 1)

    def meet_plane(count):
        @pl.when(core == 0)
        def _():
            pl.semaphore_wait(barrier, count)
            pl.semaphore_signal(go, inc=1, device_id=partner, device_id_type=MESH)

        @pl.when(core == 1)
        def _():
            pl.semaphore_wait(go, 1)

    def exchange():
        for k in range(N):
            remote(own.at[1 - core, rows(k)], part.at[rows(k)], ex_send, ex_recv.at[min(k, 1)], partner).start()

    def columns(group, head, count=1):
        return pl.ds(pl.multiple_of(group * (GROUP * DIM) + head * DIM, DIM), count * DIM)

    def states(group, k):
        first, count = CHUNKS[k]
        for head in range(first, first + count):
            at = columns(group, head)
            own[group, pl.ds(head * DIM, DIM), :] = dot(k_ref[:, at], v_ref[:, at], ((0,), (0,)))

    with scope("b_load"):
        loads[0].wait()
        loads[1].wait()
    with scope("b_states"):
        for k in range(N):
            states(1 - core, k)
            states(core, k)
    with scope("c_barrier"):
        @pl.when(jnp.logical_not(late))
        def _():
            meet_above(z_peers + 1)
            exchange()
            meet_plane(2 * (PLANE - 1))

        @pl.when(late)
        def _():
            meet_plane(2 * (PLANE - 1) + 1)
            exchange()

    for k in range(N):
        with scope(f"f_exwait{k}"):
            if k < 2:
                rest = GROUP - CHUNKS[k][0] if k else CHUNKS[0][1]
                arrived(part.at[pl.ds(CHUNKS[k][0] * DIM, rest * DIM)], ex_recv.at[k])
        with scope(f"f_up{k}"):
            total[rows(k)] = own[core, rows(k)] + part[rows(k)]
            up[slice_of(k, here)] = total[slice_of(k, here)]
            for root in others:
                remote(total.at[slice_of(k, root)], up.at[slice_of(k, here)], up_send, up_recv.at[k],
                       (chip_in_plane(root), core)).start()

    with scope("g_local"):
        loads[2].wait()
        causal = lax.broadcasted_iota(jnp.int32, (DIM, DIM), 0) >= lax.broadcasted_iota(jnp.int32, (DIM, DIM), 1)
        for head in range(HEADS):
            at = pl.ds(head * DIM, DIM)
            scores = dot(q_ref[:, at], k_ref[:, at], ((1,), (1,)))
            scores = jnp.where(causal, scores, 0.0).astype(jnp.bfloat16)
            local[:, at] = dot(scores, v_ref[:, at], ((1,), (0,)))

    with scope("g_meet"):
        @pl.when(late)
        def _():
            meet_above(z_peers)

    def to_plane(source, k, to):
        return remote(source.at[root_rows(k)], zrecv.at[z, root_rows(k)], z_send, z_recv.at[k],
                      (to * PLANE + here, core))

    def root(k):
        with scope(f"h_upwait{k}"):
            arrived(up.at[all_but_one(k)], up_recv.at[k])
        with scope(f"h_root{k}"):
            before = jnp.zeros((CHUNKS[k][1] * PIECE, DIM), jnp.float32)
            for i in range(PLANE):
                prefix[slice_of(k, i)] = before
                before = before + up[slice_of(k, i)]
            plane[root_rows(k)] = before

            @pl.loop(z + 1, z_last)
            def _(to):
                to_plane(plane, k, to).start()

    def planes_arrived(count, at, sem):
        for n in range(1, NZ - 1):
            @pl.when(count == n)
            def _():
                arrived(zrecv.at[pl.ds(0, n), at], sem)

    def earlier(k):
        with scope(f"i_zwait{k}"):
            planes_arrived(z - z_first, root_rows(k), z_recv.at[k])
            below[root_rows(k)] = lax.fori_loop(z_first, z, lambda frm, acc: acc + zrecv[frm, root_rows(k)],
                                                jnp.zeros((CHUNKS[k][1] * PIECE, DIM), jnp.float32))

        @pl.when(z == 1)
        def _():
            pair[root_rows(k)] = below[root_rows(k)] + plane[root_rows(k)]
            for to in range(HALF, NZ):
                to_plane(pair, k, to).start()

    def carries(k):
        with scope(f"i_down{k}"):
            above = below[root_rows(k)]
            for i in range(PLANE):
                down[slice_of(k, i)] = prefix[slice_of(k, i)] + above
            carry[slice_of(k, here)] = down[slice_of(k, here)]
            for chip in others:
                remote(down.at[slice_of(k, chip)], carry.at[slice_of(k, here)], dn_send, dn_recv.at[k],
                       (chip_in_plane(chip), core)).start()

    for step in range(N + max(LAGS)):
        if step < N:
            root(step)
        for lag in sorted(set(LAGS)):
            if 0 <= step - lag < N:
                wanted = [i for i in range(NZ) if LAGS[i] == lag]

                @pl.when(functools.reduce(jnp.logical_or, [z == i for i in wanted]))
                def _():
                    earlier(step - lag)
                    carries(step - lag)

    def finish(group, head, state):
        at = columns(group, head)
        high = state.astype(jnp.bfloat16)
        low = (state - high.astype(jnp.float32)).astype(jnp.bfloat16)
        q = q_ref[:, at]
        whole = local[:, at] + (dot(q, high, ((1,), (0,))) + dot(q, low, ((1,), (0,))))
        factor = lax.rsqrt(jnp.mean(whole * whole, axis=-1, keepdims=True) + 1e-05)
        o_ref[:, at] = (whole * factor).astype(jnp.bfloat16)

    def finish_other(k):
        with scope(f"k_fxwait{k}"):
            arrived(other.at[rows(k)], fx_recv.at[k])
        with scope(f"k_fin{k}"):
            first, count = CHUNKS[k]
            for head in range(first, first + count):
                finish(1 - core, head, other[pl.ds(head * DIM, DIM)])

    for k in range(N):
        with scope(f"j_dnwait{k}"):
            arrived(carry.at[all_but_one(k)], dn_recv.at[k])
        with scope(f"j_fin{k}"):
            give[rows(k)] = carry[rows(k)] + jnp.where(core == 0, own[core, rows(k)], 0.0)
            remote(give.at[rows(k)], other.at[rows(k)], fx_send, fx_recv.at[k], partner).start()
            first, count = CHUNKS[k]
            for head in range(first, first + count):
                at = pl.ds(head * DIM, DIM)
                finish(core, head, carry[at] + jnp.where(core == 0, 0.0, part[at]))
        if k:
            finish_other(k - 1)
    finish_other(N - 1)

    with scope("l_waits"):
        arrived(own.at[1 - core], ex_send)
        arrived(total.at[pl.ds(0, (PLANE - 1) * GROUP * PIECE)], up_send)
        arrived(down.at[pl.ds(0, (PLANE - 1) * GROUP * PIECE)], dn_send)
        arrived(give, fx_send)
        planes_arrived(z_last - 1 - z + jnp.where(z == 1, NZ - HALF, 0), pl.ds(0, GROUP * PIECE), z_send)


def shards(queries, keys, values):
    dma = pltpu.SemaphoreType.DMA
    hbm = pl.BlockSpec(memory_space=pltpu.HBM)
    block = pltpu.VMEM(queries.shape, queries.dtype)
    state = pltpu.VMEM((GROUP * DIM, DIM), jnp.float32)
    root = pltpu.VMEM((GROUP * PIECE, DIM), jnp.float32)
    return pl.pallas_call(
        kernel,
        out_shape=pltpu.VMEM(queries.shape, queries.dtype),
        in_specs=[hbm] * 3,
        out_specs=pl.BlockSpec(memory_space=pltpu.VMEM),
        scratch_shapes=[
            block, block, block,
            pltpu.VMEM((2, GROUP * DIM, DIM), jnp.float32),
            state, state, state, state, root, root, root,
            pltpu.VMEM((NZ, GROUP * PIECE, DIM), jnp.float32),
            state, state, state, state,
            pltpu.VMEM((DIM, HEADS * DIM), jnp.float32),
            dma((3,)), pltpu.SemaphoreType.REGULAR, pltpu.SemaphoreType.REGULAR,
            dma, dma((2,)), dma, dma((N,)), dma, dma((N,)), dma, dma((N,)), dma, dma((N,)),
        ],
        compiler_params=pltpu.CompilerParams(collective_id=0, has_side_effects=True),
        name="prefix_attention",
    )(*(pltpu.with_memory_space_constraint(x, pltpu.HBM) for x in (queries, keys, values)))


def solution(mesh):
    placed = P(("wide", "narrow"), None)
    return jax.shard_map(shards, mesh=mesh, in_specs=(placed,) * 3, out_specs=placed, check_vma=False)
```

```python
import contextlib
import functools

import jax
import jax.numpy as jnp
from jax import lax
from jax.experimental import pallas as pl
from jax.experimental.pallas import tpu as pltpu
from jax.sharding import PartitionSpec as P

HEADS = 16
DIM = 128
GROUP = HEADS // 2
CHUNKS = ((0, 2), (2, 2), (4, 2), (6, 1), (7, 1))
N = len(CHUNKS)
NZ = 8
HALF = NZ // 2
PLANE = 16
PIECE = DIM // PLANE
LAGS = (0, 1, 1, 2, 2, 2, 2, 2)
SIDE = 4
STEPS = sorted(((dx, dy) for dy in range(SIDE) for dx in range(SIDE) if dx or dy),
               key=lambda step: -sum(min(d, SIDE - d) for d in step))
MESH = pl.DeviceIdType.MESH


def scope(name):
    return contextlib.nullcontext()


def dot(a, b, dims):
    return lax.dot_general(a, b, (dims, ((), ())), preferred_element_type=jnp.float32)


def kernel(q_hbm, k_hbm, v_hbm, o_ref, q_ref, k_ref, v_ref, own, part, total, up, prefix, plane, below, pair, zrecv, down,
           carry, give, other, local, in_sem, hello, go,
           ex_send, ex_recv, up_send, up_recv, z_send, z_recv, dn_send, dn_recv, fx_send, fx_recv):
    wide, core = lax.axis_index("wide"), lax.axis_index("narrow")
    here = wide % PLANE
    z = wide // PLANE
    x, y = here % SIDE, here // SIDE
    others = [(y + dy) % SIDE * SIDE + (x + dx) % SIDE for dx, dy in STEPS]
    partner = (wide, 1 - core)
    z_first = jnp.where(z < HALF, 0, 1)
    z_last = jnp.where(z < 2, HALF, NZ)

    def chip_in_plane(i):
        return z * PLANE + i

    def remote(src, dst, send, recv, to):
        return pltpu.make_async_remote_copy(src, dst, send, recv, device_id=to, device_id_type=MESH)

    def arrived(ref, sem):
        pltpu.make_async_copy(ref, ref, sem).wait()

    def rows(k):
        first, count = CHUNKS[k]
        return pl.ds(first * DIM, count * DIM)

    def slice_of(k, i):
        first, count = CHUNKS[k]
        return pl.ds(pl.multiple_of(first * DIM + i * (count * PIECE), 8), count * PIECE)

    def root_rows(k):
        first, count = CHUNKS[k]
        return pl.ds(first * PIECE, count * PIECE)

    def all_but_one(k):
        first, count = CHUNKS[k]
        return pl.ds(first * DIM, (PLANE - 1) * count * PIECE)

    with scope("a_sig"):
        barrier = pltpu.get_barrier_semaphore()
        late = jnp.where(z == 0, x + y > 1, jnp.where(z == 3, x + y > 2, (z < HALF) | ((z == HALF) & (x >= 2) & (y >= 2))))

        @pl.when(jnp.where(late, 1, 0) == core)
        def _():
            pl.semaphore_signal(barrier, inc=1, device_id=partner, device_id_type=MESH)

        for chip in others:
            pl.semaphore_signal(barrier, inc=1, device_id=(chip_in_plane(chip), 0), device_id_type=MESH)

        @pl.when(core == 1)
        def _():
            @pl.loop(z_first, z)
            def _(frm):
                pl.semaphore_signal(barrier, inc=1, device_id=(frm * PLANE + here, 1), device_id_type=MESH)

        loads = [pltpu.make_async_copy(src, dst, in_sem.at[i])
                 for i, (src, dst) in enumerate(((k_hbm, k_ref), (v_hbm, v_ref), (q_hbm, q_ref)))]
        for load in loads:
            load.start()

    z_peers = z_last - 1 - z + jnp.where(z == 1, NZ - HALF, 0)

    def meet_above(count):
        @pl.when(core == 1)
        def _():
            pl.semaphore_wait(barrier, count)
            pl.semaphore_signal(hello, inc=1, device_id=partner, device_id_type=MESH)

        @pl.when(core == 0)
        def _():
            pl.semaphore_wait(hello, 1)

    def meet_plane(count):
        @pl.when(core == 0)
        def _():
            pl.semaphore_wait(barrier, count)
            pl.semaphore_signal(go, inc=1, device_id=partner, device_id_type=MESH)

        @pl.when(core == 1)
        def _():
            pl.semaphore_wait(go, 1)

    def exchange():
        for k in range(N):
            remote(own.at[1 - core, rows(k)], part.at[rows(k)], ex_send, ex_recv.at[min(k, 1)], partner).start()

    def columns(group, head, count=1):
        return pl.ds(pl.multiple_of(group * (GROUP * DIM) + head * DIM, DIM), count * DIM)

    def states(group, k):
        first, count = CHUNKS[k]
        for head in range(first, first + count):
            at = columns(group, head)
            own[group, pl.ds(head * DIM, DIM), :] = dot(k_ref[:, at], v_ref[:, at], ((0,), (0,)))

    with scope("b_load"):
        loads[0].wait()
        loads[1].wait()
    with scope("b_states"):
        for k in range(N):
            states(1 - core, k)
            states(core, k)
    with scope("c_barrier"):
        @pl.when(jnp.logical_not(late))
        def _():
            meet_above(z_peers + 1)
            exchange()
            meet_plane(2 * (PLANE - 1))

        @pl.when(late)
        def _():
            meet_plane(2 * (PLANE - 1) + 1)
            exchange()

    for k in range(N):
        with scope(f"f_exwait{k}"):
            if k < 2:
                rest = GROUP - CHUNKS[k][0] if k else CHUNKS[0][1]
                arrived(part.at[pl.ds(CHUNKS[k][0] * DIM, rest * DIM)], ex_recv.at[k])
        with scope(f"f_up{k}"):
            total[rows(k)] = own[core, rows(k)] + part[rows(k)]
            for root in others:
                remote(total.at[slice_of(k, root)], up.at[core, slice_of(k, here)], up_send, up_recv.at[core, k],
                       (chip_in_plane(root), 1)).start()

            @pl.when(core == 0)
            def _():
                remote(total.at[slice_of(k, here)], up.at[0, slice_of(k, here)], up_send, up_recv.at[0, k], partner).start()

            @pl.when(core == 1)
            def _():
                up[1, slice_of(k, here)] = total[slice_of(k, here)]

    with scope("g_local"):
        loads[2].wait()
        causal = lax.broadcasted_iota(jnp.int32, (DIM, DIM), 0) >= lax.broadcasted_iota(jnp.int32, (DIM, DIM), 1)
        for head in range(HEADS):
            at = pl.ds(head * DIM, DIM)
            scores = dot(q_ref[:, at], k_ref[:, at], ((1,), (1,)))
            scores = jnp.where(causal, scores, 0.0).astype(jnp.bfloat16)
            local[:, at] = dot(scores, v_ref[:, at], ((1,), (0,)))

    with scope("g_meet"):
        @pl.when(late & (core == 1))
        def _():
            pl.semaphore_wait(barrier, z_peers)

    def to_plane(source, g, k, to):
        return remote(source.at[g, root_rows(k)], zrecv.at[g, z, root_rows(k)], z_send, z_recv.at[g, k],
                      (to * PLANE + here, 1))

    def root(g, k):
        with scope(f"h_upwait{k}_{g}"):
            arrived(up.at[g, all_but_one(k) if g else rows(k)], up_recv.at[g, k])
        with scope(f"h_root{k}_{g}"):
            before = jnp.zeros((CHUNKS[k][1] * PIECE, DIM), jnp.float32)
            for i in range(PLANE):
                prefix[g, slice_of(k, i)] = before
                before = before + up[g, slice_of(k, i)]
            plane[g, root_rows(k)] = before

            @pl.loop(z + 1, z_last)
            def _(to):
                to_plane(plane, g, k, to).start()

    def earlier(g, k):
        with scope(f"i_zwait{k}_{g}"):
            for n in range(1, NZ - 1):
                @pl.when(z - z_first == n)
                def _():
                    arrived(zrecv.at[g, pl.ds(0, n), root_rows(k)], z_recv.at[g, k])

            below[g, root_rows(k)] = lax.fori_loop(z_first, z, lambda frm, acc: acc + zrecv[g, frm, root_rows(k)],
                                                   jnp.zeros((CHUNKS[k][1] * PIECE, DIM), jnp.float32))

        @pl.when(z == 1)
        def _():
            pair[g, root_rows(k)] = below[g, root_rows(k)] + plane[g, root_rows(k)]
            for to in range(HALF, NZ):
                to_plane(pair, g, k, to).start()

    def carries(g, k):
        with scope(f"i_down{k}_{g}"):
            above = below[g, root_rows(k)]
            for i in range(PLANE):
                down[g, slice_of(k, i)] = prefix[g, slice_of(k, i)] + above
            for chip in others:
                remote(down.at[g, slice_of(k, chip)], carry.at[slice_of(k, here)], dn_send, dn_recv.at[k],
                       (chip_in_plane(chip), g)).start()
            if g:
                carry[slice_of(k, here)] = down[g, slice_of(k, here)]
            else:
                remote(down.at[g, slice_of(k, here)], carry.at[slice_of(k, here)], dn_send, dn_recv.at[k], partner).start()

    @pl.when(core == 1)
    def _():
        for step in range(N + max(LAGS)):
            if step < N:
                for g in (1, 0):
                    root(g, step)
            for lag in sorted(set(LAGS)):
                if 0 <= step - lag < N:
                    wanted = [i for i in range(NZ) if LAGS[i] == lag]

                    @pl.when(functools.reduce(jnp.logical_or, [z == i for i in wanted]))
                    def _():
                        for g in (1, 0):
                            earlier(g, step - lag)
                            carries(g, step - lag)

    def finish(group, head, state):
        at = columns(group, head)
        high = state.astype(jnp.bfloat16)
        low = (state - high.astype(jnp.float32)).astype(jnp.bfloat16)
        q = q_ref[:, at]
        whole = local[:, at] + (dot(q, high, ((1,), (0,))) + dot(q, low, ((1,), (0,))))
        factor = lax.rsqrt(jnp.mean(whole * whole, axis=-1, keepdims=True) + 1e-05)
        o_ref[:, at] = (whole * factor).astype(jnp.bfloat16)

    def finish_other(k):
        with scope(f"k_fxwait{k}"):
            arrived(other.at[rows(k)], fx_recv.at[k])
        with scope(f"k_fin{k}"):
            first, count = CHUNKS[k]
            for head in range(first, first + count):
                finish(1 - core, head, other[pl.ds(head * DIM, DIM)])

    for k in range(N):
        with scope(f"j_dnwait{k}"):
            @pl.when(core == 0)
            def _():
                arrived(carry.at[rows(k)], dn_recv.at[k])

            @pl.when(core == 1)
            def _():
                arrived(carry.at[all_but_one(k)], dn_recv.at[k])
        with scope(f"j_fin{k}"):
            give[rows(k)] = carry[rows(k)] + jnp.where(core == 0, own[core, rows(k)], 0.0)
            remote(give.at[rows(k)], other.at[rows(k)], fx_send, fx_recv.at[k], partner).start()
            first, count = CHUNKS[k]
            for head in range(first, first + count):
                at = pl.ds(head * DIM, DIM)
                finish(core, head, carry[at] + jnp.where(core == 0, 0.0, part[at]))
        if k:
            finish_other(k - 1)
    finish_other(N - 1)

    with scope("l_waits"):
        arrived(own.at[1 - core], ex_send)
        @pl.when(core == 0)
        def _():
            arrived(total, up_send)

        arrived(give, fx_send)

        @pl.when(core == 1)
        def _():
            most = (PLANE - 1) * GROUP * PIECE
            arrived(total.at[pl.ds(0, most)], up_send)
            arrived(down.reshape(2 * GROUP * DIM, DIM).at[pl.ds(0, GROUP * DIM + most)], dn_send)
            for n in range(1, NZ - 1):
                @pl.when(z_peers == n)
                def _():
                    arrived(zrecv.at[:, pl.ds(0, n)], z_send)


def shards(queries, keys, values):
    dma = pltpu.SemaphoreType.DMA
    hbm = pl.BlockSpec(memory_space=pltpu.HBM)
    block = pltpu.VMEM(queries.shape, queries.dtype)
    state = pltpu.VMEM((GROUP * DIM, DIM), jnp.float32)
    states = pltpu.VMEM((2, GROUP * DIM, DIM), jnp.float32)
    root = pltpu.VMEM((2, GROUP * PIECE, DIM), jnp.float32)
    return pl.pallas_call(
        kernel,
        out_shape=pltpu.VMEM(queries.shape, queries.dtype),
        in_specs=[hbm] * 3,
        out_specs=pl.BlockSpec(memory_space=pltpu.VMEM),
        scratch_shapes=[
            block, block, block,
            states, state, state, states, states, root, root, root,
            pltpu.VMEM((2, NZ, GROUP * PIECE, DIM), jnp.float32),
            states, state, state, state,
            pltpu.VMEM((DIM, HEADS * DIM), jnp.float32),
            dma((3,)), pltpu.SemaphoreType.REGULAR, pltpu.SemaphoreType.REGULAR,
            dma, dma((2,)), dma, dma((2, N)), dma, dma((2, N)), dma, dma((N,)), dma, dma((N,)),
        ],
        compiler_params=pltpu.CompilerParams(collective_id=0, has_side_effects=True),
        name="prefix_attention",
    )(*(pltpu.with_memory_space_constraint(x, pltpu.HBM) for x in (queries, keys, values)))


def solution(mesh):
    placed = P(("wide", "narrow"), None)
    return jax.shard_map(shards, mesh=mesh, in_specs=(placed,) * 3, out_specs=placed, check_vma=False)
```

```python
import contextlib
import functools

import jax
import jax.numpy as jnp
from jax import lax
from jax.experimental import pallas as pl
from jax.experimental.pallas import tpu as pltpu
from jax.sharding import PartitionSpec as P

HEADS = 16
DIM = 128
GROUP = HEADS // 2
CHUNKS = ((0, 2), (2, 2), (4, 2), (6, 1), (7, 1))
N = len(CHUNKS)
NZ = 8
HALF = NZ // 2
PLANE = 16
PIECE = DIM // PLANE
LAGS = (0, 1, 1, 1, 2, 2, 2, 2)
SIDE = 4
STEPS = sorted(((dx, dy) for dy in range(SIDE) for dx in range(SIDE) if dx or dy),
               key=lambda step: -sum(min(d, SIDE - d) for d in step))
MESH = pl.DeviceIdType.MESH


def scope(name):
    return contextlib.nullcontext()


def dot(a, b, dims):
    return lax.dot_general(a, b, (dims, ((), ())), preferred_element_type=jnp.float32)


def kernel(q_hbm, k_hbm, v_hbm, o_ref, q_ref, k_ref, v_ref, own, part, total, up, prefix, plane, below, pair, zrecv, down,
           carry, give, other, local, in_sem, hello, go,
           ex_send, ex_recv, up_send, up_recv, z_send, z_recv, dn_send, dn_recv, fx_send, fx_recv):
    wide, core = lax.axis_index("wide"), lax.axis_index("narrow")
    here = wide % PLANE
    z = wide // PLANE
    x, y = here % SIDE, here // SIDE
    others = [(y + dy) % SIDE * SIDE + (x + dx) % SIDE for dx, dy in STEPS]
    partner = (wide, 1 - core)
    z_first = jnp.where(z < HALF, 0, 1)
    z_last = jnp.where(z < 2, HALF, NZ)

    def chip_in_plane(i):
        return z * PLANE + i

    def remote(src, dst, send, recv, to):
        return pltpu.make_async_remote_copy(src, dst, send, recv, device_id=to, device_id_type=MESH)

    def arrived(ref, sem):
        pltpu.make_async_copy(ref, ref, sem).wait()

    def rows(k):
        first, count = CHUNKS[k]
        return pl.ds(first * DIM, count * DIM)

    def slice_of(k, i):
        first, count = CHUNKS[k]
        return pl.ds(pl.multiple_of(first * DIM + i * (count * PIECE), 8), count * PIECE)

    def root_rows(k):
        first, count = CHUNKS[k]
        return pl.ds(first * PIECE, count * PIECE)

    def all_but_one(k):
        first, count = CHUNKS[k]
        return pl.ds(first * DIM, (PLANE - 1) * count * PIECE)

    with scope("a_sig"):
        barrier = pltpu.get_barrier_semaphore()
        late = jnp.where(z == 0, x + y > 1, jnp.where(z == 3, x + y > 2, (z < HALF) | ((z == HALF) & (x >= 2) & (y >= 2))))

        @pl.when(jnp.where(late, 1, 0) == core)
        def _():
            pl.semaphore_signal(barrier, inc=1, device_id=partner, device_id_type=MESH)

        for chip in others:
            pl.semaphore_signal(barrier, inc=1, device_id=(chip_in_plane(chip), 0), device_id_type=MESH)

        @pl.when(core == 1)
        def _():
            @pl.loop(z_first, z)
            def _(frm):
                pl.semaphore_signal(barrier, inc=1, device_id=(frm * PLANE + here, 1), device_id_type=MESH)

        loads = [pltpu.make_async_copy(src, dst, in_sem.at[i])
                 for i, (src, dst) in enumerate(((k_hbm, k_ref), (v_hbm, v_ref), (q_hbm, q_ref)))]
        for load in loads:
            load.start()

    z_peers = z_last - 1 - z + jnp.where(z == 1, NZ - HALF, 0)

    def meet_above(count):
        @pl.when(core == 1)
        def _():
            pl.semaphore_wait(barrier, count)
            pl.semaphore_signal(hello, inc=1, device_id=partner, device_id_type=MESH)

        @pl.when(core == 0)
        def _():
            pl.semaphore_wait(hello, 1)

    def meet_plane(count):
        @pl.when(core == 0)
        def _():
            pl.semaphore_wait(barrier, count)
            pl.semaphore_signal(go, inc=1, device_id=partner, device_id_type=MESH)

        @pl.when(core == 1)
        def _():
            pl.semaphore_wait(go, 1)

    def exchange():
        for k in range(N):
            remote(own.at[1 - core, rows(k)], part.at[rows(k)], ex_send, ex_recv.at[min(k, 1)], partner).start()

    def columns(group, head, count=1):
        return pl.ds(pl.multiple_of(group * (GROUP * DIM) + head * DIM, DIM), count * DIM)

    def states(group, k):
        first, count = CHUNKS[k]
        for head in range(first, first + count):
            at = columns(group, head)
            own[group, pl.ds(head * DIM, DIM), :] = dot(k_ref[:, at], v_ref[:, at], ((0,), (0,)))

    with scope("b_load"):
        loads[0].wait()
        loads[1].wait()
    with scope("b_states"):
        for k in range(N):
            states(1 - core, k)
            states(core, k)
    with scope("c_barrier"):
        @pl.when(jnp.logical_not(late))
        def _():
            meet_above(z_peers + 1)
            exchange()
            meet_plane(2 * (PLANE - 1))

        @pl.when(late)
        def _():
            meet_plane(2 * (PLANE - 1) + 1)
            exchange()

    for k in range(N):
        with scope(f"f_exwait{k}"):
            if k < 2:
                rest = GROUP - CHUNKS[k][0] if k else CHUNKS[0][1]
                arrived(part.at[pl.ds(CHUNKS[k][0] * DIM, rest * DIM)], ex_recv.at[k])
        with scope(f"f_up{k}"):
            total[rows(k)] = own[core, rows(k)] + part[rows(k)]
            for root in others:
                remote(total.at[slice_of(k, root)], up.at[core, slice_of(k, here)], up_send, up_recv.at[core, k],
                       (chip_in_plane(root), 1)).start()

            @pl.when(core == 0)
            def _():
                remote(total.at[slice_of(k, here)], up.at[0, slice_of(k, here)], up_send, up_recv.at[0, k], partner).start()

            @pl.when(core == 1)
            def _():
                up[1, slice_of(k, here)] = total[slice_of(k, here)]

    with scope("g_local"):
        loads[2].wait()
        causal = lax.broadcasted_iota(jnp.int32, (DIM, DIM), 0) >= lax.broadcasted_iota(jnp.int32, (DIM, DIM), 1)
        for head in range(HEADS):
            at = pl.ds(head * DIM, DIM)
            scores = dot(q_ref[:, at], k_ref[:, at], ((1,), (1,)))
            scores = jnp.where(causal, scores, 0.0).astype(jnp.bfloat16)
            local[:, at] = dot(scores, v_ref[:, at], ((1,), (0,)))

    with scope("g_meet"):
        @pl.when(late & (core == 1))
        def _():
            pl.semaphore_wait(barrier, z_peers)

    def to_plane(source, g, k, to):
        return remote(source.at[g, root_rows(k)], zrecv.at[g, z, root_rows(k)], z_send, z_recv.at[g, k],
                      (to * PLANE + here, 1))

    def root(g, k):
        with scope(f"h_upwait{k}_{g}"):
            arrived(up.at[g, all_but_one(k) if g else rows(k)], up_recv.at[g, k])
        with scope(f"h_root{k}_{g}"):
            before = jnp.zeros((CHUNKS[k][1] * PIECE, DIM), jnp.float32)
            for i in range(PLANE):
                prefix[g, slice_of(k, i)] = before
                before = before + up[g, slice_of(k, i)]
            plane[g, root_rows(k)] = before

            @pl.loop(z + 1, z_last)
            def _(to):
                to_plane(plane, g, k, to).start()

    def earlier(g, k):
        with scope(f"i_zwait{k}_{g}"):
            for n in range(1, NZ - 1):
                @pl.when(z - z_first == n)
                def _():
                    arrived(zrecv.at[g, pl.ds(0, n), root_rows(k)], z_recv.at[g, k])

            below[g, root_rows(k)] = lax.fori_loop(z_first, z, lambda frm, acc: acc + zrecv[g, frm, root_rows(k)],
                                                   jnp.zeros((CHUNKS[k][1] * PIECE, DIM), jnp.float32))

        @pl.when(z == 1)
        def _():
            pair[g, root_rows(k)] = below[g, root_rows(k)] + plane[g, root_rows(k)]
            for to in range(HALF, NZ):
                to_plane(pair, g, k, to).start()

    def carries(g, k):
        with scope(f"i_down{k}_{g}"):
            above = below[g, root_rows(k)]
            for i in range(PLANE):
                down[g, slice_of(k, i)] = prefix[g, slice_of(k, i)] + above
            for chip in others:
                remote(down.at[g, slice_of(k, chip)], carry.at[slice_of(k, here)], dn_send, dn_recv.at[k],
                       (chip_in_plane(chip), g)).start()
            if g:
                carry[slice_of(k, here)] = down[g, slice_of(k, here)]
            else:
                remote(down.at[g, slice_of(k, here)], carry.at[slice_of(k, here)], dn_send, dn_recv.at[k], partner).start()

    @pl.when(core == 1)
    def _():
        for step in range(N + max(LAGS)):
            if step < N:
                for g in (1, 0):
                    root(g, step)
            for lag in sorted(set(LAGS)):
                if 0 <= step - lag < N:
                    wanted = [i for i in range(NZ) if LAGS[i] == lag]

                    @pl.when(functools.reduce(jnp.logical_or, [z == i for i in wanted]))
                    def _():
                        for g in (1, 0):
                            earlier(g, step - lag)
                            carries(g, step - lag)

    def finish(group, head, state):
        at = columns(group, head)
        high = state.astype(jnp.bfloat16)
        low = (state - high.astype(jnp.float32)).astype(jnp.bfloat16)
        q = q_ref[:, at]
        whole = local[:, at] + (dot(q, high, ((1,), (0,))) + dot(q, low, ((1,), (0,))))
        factor = lax.rsqrt(jnp.mean(whole * whole, axis=-1, keepdims=True) + 1e-05)
        o_ref[:, at] = (whole * factor).astype(jnp.bfloat16)

    def finish_other(k):
        with scope(f"k_fxwait{k}"):
            arrived(other.at[rows(k)], fx_recv.at[k])
        with scope(f"k_fin{k}"):
            first, count = CHUNKS[k]
            for head in range(first, first + count):
                finish(1 - core, head, other[pl.ds(head * DIM, DIM)])

    for k in range(N):
        with scope(f"j_dnwait{k}"):
            @pl.when(core == 0)
            def _():
                arrived(carry.at[rows(k)], dn_recv.at[k])

            @pl.when(core == 1)
            def _():
                arrived(carry.at[all_but_one(k)], dn_recv.at[k])
        with scope(f"j_fin{k}"):
            give[rows(k)] = carry[rows(k)] + jnp.where(core == 0, own[core, rows(k)], 0.0)
            remote(give.at[rows(k)], other.at[rows(k)], fx_send, fx_recv.at[k], partner).start()
            first, count = CHUNKS[k]
            for head in range(first, first + count):
                at = pl.ds(head * DIM, DIM)
                finish(core, head, carry[at] + jnp.where(core == 0, 0.0, part[at]))
        if k:
            finish_other(k - 1)
    finish_other(N - 1)

    with scope("l_waits"):
        arrived(own.at[1 - core], ex_send)
        @pl.when(core == 0)
        def _():
            arrived(total, up_send)

        arrived(give, fx_send)

        @pl.when(core == 1)
        def _():
            most = (PLANE - 1) * GROUP * PIECE
            arrived(total.at[pl.ds(0, most)], up_send)
            arrived(down.reshape(2 * GROUP * DIM, DIM).at[pl.ds(0, GROUP * DIM + most)], dn_send)
            for n in range(1, NZ - 1):
                @pl.when(z_peers == n)
                def _():
                    arrived(zrecv.at[:, pl.ds(0, n)], z_send)


def shards(queries, keys, values):
    dma = pltpu.SemaphoreType.DMA
    hbm = pl.BlockSpec(memory_space=pltpu.HBM)
    block = pltpu.VMEM(queries.shape, queries.dtype)
    state = pltpu.VMEM((GROUP * DIM, DIM), jnp.float32)
    states = pltpu.VMEM((2, GROUP * DIM, DIM), jnp.float32)
    root = pltpu.VMEM((2, GROUP * PIECE, DIM), jnp.float32)
    return pl.pallas_call(
        kernel,
        out_shape=pltpu.VMEM(queries.shape, queries.dtype),
        in_specs=[hbm] * 3,
        out_specs=pl.BlockSpec(memory_space=pltpu.VMEM),
        scratch_shapes=[
            block, block, block,
            states, state, state, states, states, root, root, root,
            pltpu.VMEM((2, NZ, GROUP * PIECE, DIM), jnp.float32),
            states, state, state, state,
            pltpu.VMEM((DIM, HEADS * DIM), jnp.float32),
            dma((3,)), pltpu.SemaphoreType.REGULAR, pltpu.SemaphoreType.REGULAR,
            dma, dma((2,)), dma, dma((2, N)), dma, dma((2, N)), dma, dma((N,)), dma, dma((N,)),
        ],
        compiler_params=pltpu.CompilerParams(collective_id=0, has_side_effects=True),
        name="prefix_attention",
    )(*(pltpu.with_memory_space_constraint(x, pltpu.HBM) for x in (queries, keys, values)))


def solution(mesh):
    placed = P(("wide", "narrow"), None)
    return jax.shard_map(shards, mesh=mesh, in_specs=(placed,) * 3, out_specs=placed, check_vma=False)
```

```python
import contextlib
import functools

import jax
import jax.numpy as jnp
from jax import lax
from jax.experimental import pallas as pl
from jax.experimental.pallas import tpu as pltpu
from jax.sharding import PartitionSpec as P

HEADS = 16
DIM = 128
GROUP = HEADS // 2
CHUNKS = ((0, 1), (1, 2), (3, 2), (5, 2), (7, 1))
N = len(CHUNKS)
NZ = 8
HALF = NZ // 2
PLANE = 16
PIECE = DIM // PLANE
LAGS = (0, 1, 1, 1, 2, 2, 2, 2)
SIDE = 4
STEPS = sorted(((dx, dy) for dy in range(SIDE) for dx in range(SIDE) if dx or dy),
               key=lambda step: -sum(min(d, SIDE - d) for d in step))
MESH = pl.DeviceIdType.MESH


def scope(name):
    return contextlib.nullcontext()


def dot(a, b, dims):
    return lax.dot_general(a, b, (dims, ((), ())), preferred_element_type=jnp.float32)


def kernel(q_hbm, k_hbm, v_hbm, o_ref, q_ref, k_ref, v_ref, own, part, total, up, prefix, plane, below, pair, zrecv, down,
           carry, give, other, local, in_sem, hello, go,
           ex_send, ex_recv, up_send, up_recv, z_send, z_recv, dn_send, dn_recv, fx_send, fx_recv):
    wide, core = lax.axis_index("wide"), lax.axis_index("narrow")
    here = wide % PLANE
    z = wide // PLANE
    x, y = here % SIDE, here // SIDE
    others = [(y + dy) % SIDE * SIDE + (x + dx) % SIDE for dx, dy in STEPS]
    partner = (wide, 1 - core)
    z_first = jnp.where(z < HALF, 0, 1)
    z_last = jnp.where(z < 2, HALF, NZ)

    def chip_in_plane(i):
        return z * PLANE + i

    def remote(src, dst, send, recv, to):
        return pltpu.make_async_remote_copy(src, dst, send, recv, device_id=to, device_id_type=MESH)

    def arrived(ref, sem):
        pltpu.make_async_copy(ref, ref, sem).wait()

    def rows(k):
        first, count = CHUNKS[k]
        return pl.ds(first * DIM, count * DIM)

    def slice_of(k, i):
        first, count = CHUNKS[k]
        return pl.ds(pl.multiple_of(first * DIM + i * (count * PIECE), 8), count * PIECE)

    def root_rows(k):
        first, count = CHUNKS[k]
        return pl.ds(first * PIECE, count * PIECE)

    def all_but_one(k):
        first, count = CHUNKS[k]
        return pl.ds(first * DIM, (PLANE - 1) * count * PIECE)

    with scope("a_sig"):
        barrier = pltpu.get_barrier_semaphore()
        late = jnp.where(z == 0, x + y > 1, jnp.where(z == 3, x + y > 2, (z < HALF) | ((z == HALF) & (x >= 2) & (y >= 2))))

        @pl.when(jnp.where(late, 1, 0) == core)
        def _():
            pl.semaphore_signal(barrier, inc=1, device_id=partner, device_id_type=MESH)

        for chip in others:
            pl.semaphore_signal(barrier, inc=1, device_id=(chip_in_plane(chip), 0), device_id_type=MESH)

        @pl.when(core == 1)
        def _():
            @pl.loop(z_first, z)
            def _(frm):
                pl.semaphore_signal(barrier, inc=1, device_id=(frm * PLANE + here, 1), device_id_type=MESH)

        loads = [pltpu.make_async_copy(src, dst, in_sem.at[i])
                 for i, (src, dst) in enumerate(((k_hbm, k_ref), (v_hbm, v_ref), (q_hbm, q_ref)))]
        for load in loads:
            load.start()

    z_peers = z_last - 1 - z + jnp.where(z == 1, NZ - HALF, 0)

    def meet_above(count):
        @pl.when(core == 1)
        def _():
            pl.semaphore_wait(barrier, count)
            pl.semaphore_signal(hello, inc=1, device_id=partner, device_id_type=MESH)

        @pl.when(core == 0)
        def _():
            pl.semaphore_wait(hello, 1)

    def meet_plane(count):
        @pl.when(core == 0)
        def _():
            pl.semaphore_wait(barrier, count)
            pl.semaphore_signal(go, inc=1, device_id=partner, device_id_type=MESH)

        @pl.when(core == 1)
        def _():
            pl.semaphore_wait(go, 1)

    def exchange():
        for k in range(N):
            remote(own.at[1 - core, rows(k)], part.at[rows(k)], ex_send, ex_recv.at[min(k, 1)], partner).start()

    def columns(group, head, count=1):
        return pl.ds(pl.multiple_of(group * (GROUP * DIM) + head * DIM, DIM), count * DIM)

    def states(group, k):
        first, count = CHUNKS[k]
        for head in range(first, first + count):
            at = columns(group, head)
            own[group, pl.ds(head * DIM, DIM), :] = dot(k_ref[:, at], v_ref[:, at], ((0,), (0,)))

    with scope("b_load"):
        loads[0].wait()
        loads[1].wait()
    with scope("b_states"):
        for k in range(N):
            states(1 - core, k)
            states(core, k)
    with scope("c_barrier"):
        @pl.when(jnp.logical_not(late))
        def _():
            meet_above(z_peers + 1)
            exchange()
            meet_plane(2 * (PLANE - 1))

        @pl.when(late)
        def _():
            meet_plane(2 * (PLANE - 1) + 1)
            exchange()

    for k in range(N):
        with scope(f"f_exwait{k}"):
            if k < 2:
                rest = GROUP - CHUNKS[k][0] if k else CHUNKS[0][1]
                arrived(part.at[pl.ds(CHUNKS[k][0] * DIM, rest * DIM)], ex_recv.at[k])
        with scope(f"f_up{k}"):
            total[rows(k)] = own[core, rows(k)] + part[rows(k)]
            for root in others:
                remote(total.at[slice_of(k, root)], up.at[core, slice_of(k, here)], up_send, up_recv.at[core, k],
                       (chip_in_plane(root), 1)).start()

            @pl.when(core == 0)
            def _():
                remote(total.at[slice_of(k, here)], up.at[0, slice_of(k, here)], up_send, up_recv.at[0, k], partner).start()

            @pl.when(core == 1)
            def _():
                up[1, slice_of(k, here)] = total[slice_of(k, here)]

    with scope("g_local"):
        loads[2].wait()
        causal = lax.broadcasted_iota(jnp.int32, (DIM, DIM), 0) >= lax.broadcasted_iota(jnp.int32, (DIM, DIM), 1)
        for head in range(HEADS):
            at = pl.ds(head * DIM, DIM)
            scores = dot(q_ref[:, at], k_ref[:, at], ((1,), (1,)))
            scores = jnp.where(causal, scores, 0.0).astype(jnp.bfloat16)
            local[:, at] = dot(scores, v_ref[:, at], ((1,), (0,)))

    with scope("g_meet"):
        @pl.when(late & (core == 1))
        def _():
            pl.semaphore_wait(barrier, z_peers)

    def to_plane(source, g, k, to):
        return remote(source.at[g, root_rows(k)], zrecv.at[g, z, root_rows(k)], z_send, z_recv.at[g, k],
                      (to * PLANE + here, 1))

    def root(g, k):
        with scope(f"h_upwait{k}_{g}"):
            arrived(up.at[g, all_but_one(k) if g else rows(k)], up_recv.at[g, k])
        with scope(f"h_root{k}_{g}"):
            before = jnp.zeros((CHUNKS[k][1] * PIECE, DIM), jnp.float32)
            for i in range(PLANE):
                prefix[g, slice_of(k, i)] = before
                before = before + up[g, slice_of(k, i)]
            plane[g, root_rows(k)] = before

            @pl.loop(z + 1, z_last)
            def _(to):
                to_plane(plane, g, k, to).start()

    def earlier(g, k):
        with scope(f"i_zwait{k}_{g}"):
            for n in range(1, NZ - 1):
                @pl.when(z - z_first == n)
                def _():
                    arrived(zrecv.at[g, pl.ds(0, n), root_rows(k)], z_recv.at[g, k])

            below[g, root_rows(k)] = lax.fori_loop(z_first, z, lambda frm, acc: acc + zrecv[g, frm, root_rows(k)],
                                                   jnp.zeros((CHUNKS[k][1] * PIECE, DIM), jnp.float32))

        @pl.when(z == 1)
        def _():
            pair[g, root_rows(k)] = below[g, root_rows(k)] + plane[g, root_rows(k)]
            for to in range(HALF, NZ):
                to_plane(pair, g, k, to).start()

    def carries(g, k):
        with scope(f"i_down{k}_{g}"):
            above = below[g, root_rows(k)]
            for i in range(PLANE):
                down[g, slice_of(k, i)] = prefix[g, slice_of(k, i)] + above
            for chip in others:
                remote(down.at[g, slice_of(k, chip)], carry.at[slice_of(k, here)], dn_send, dn_recv.at[k],
                       (chip_in_plane(chip), g)).start()
            if g:
                carry[slice_of(k, here)] = down[g, slice_of(k, here)]
            else:
                remote(down.at[g, slice_of(k, here)], carry.at[slice_of(k, here)], dn_send, dn_recv.at[k], partner).start()

    @pl.when(core == 1)
    def _():
        for step in range(N + max(LAGS)):
            for g in (1, 0):
                if step < N:
                    root(g, step)
                for lag in sorted(set(LAGS)):
                    if 0 <= step - lag < N:
                        wanted = [i for i in range(NZ) if LAGS[i] == lag]

                        @pl.when(functools.reduce(jnp.logical_or, [z == i for i in wanted]))
                        def _():
                            earlier(g, step - lag)
                            carries(g, step - lag)

    def finish(group, head, state):
        at = columns(group, head)
        high = state.astype(jnp.bfloat16)
        low = (state - high.astype(jnp.float32)).astype(jnp.bfloat16)
        q = q_ref[:, at]
        whole = local[:, at] + (dot(q, high, ((1,), (0,))) + dot(q, low, ((1,), (0,))))
        factor = lax.rsqrt(jnp.mean(whole * whole, axis=-1, keepdims=True) + 1e-05)
        o_ref[:, at] = (whole * factor).astype(jnp.bfloat16)

    def finish_other(k):
        with scope(f"k_fxwait{k}"):
            arrived(other.at[rows(k)], fx_recv.at[k])
        with scope(f"k_fin{k}"):
            first, count = CHUNKS[k]
            for head in range(first, first + count):
                finish(1 - core, head, other[pl.ds(head * DIM, DIM)])

    for k in range(N):
        with scope(f"j_dnwait{k}"):
            @pl.when(core == 0)
            def _():
                arrived(carry.at[rows(k)], dn_recv.at[k])

            @pl.when(core == 1)
            def _():
                arrived(carry.at[all_but_one(k)], dn_recv.at[k])
        with scope(f"j_fin{k}"):
            give[rows(k)] = carry[rows(k)] + jnp.where(core == 0, own[core, rows(k)], 0.0)
            remote(give.at[rows(k)], other.at[rows(k)], fx_send, fx_recv.at[k], partner).start()
            first, count = CHUNKS[k]
            for head in range(first, first + count):
                at = pl.ds(head * DIM, DIM)
                finish(core, head, carry[at] + jnp.where(core == 0, 0.0, part[at]))
        if k:
            finish_other(k - 1)
    finish_other(N - 1)

    with scope("l_waits"):
        arrived(own.at[1 - core], ex_send)
        @pl.when(core == 0)
        def _():
            arrived(total, up_send)

        arrived(give, fx_send)

        @pl.when(core == 1)
        def _():
            most = (PLANE - 1) * GROUP * PIECE
            arrived(total.at[pl.ds(0, most)], up_send)
            arrived(down.reshape(2 * GROUP * DIM, DIM).at[pl.ds(0, GROUP * DIM + most)], dn_send)
            for n in range(1, NZ - 1):
                @pl.when(z_peers == n)
                def _():
                    arrived(zrecv.at[:, pl.ds(0, n)], z_send)


def shards(queries, keys, values):
    dma = pltpu.SemaphoreType.DMA
    hbm = pl.BlockSpec(memory_space=pltpu.HBM)
    block = pltpu.VMEM(queries.shape, queries.dtype)
    state = pltpu.VMEM((GROUP * DIM, DIM), jnp.float32)
    states = pltpu.VMEM((2, GROUP * DIM, DIM), jnp.float32)
    root = pltpu.VMEM((2, GROUP * PIECE, DIM), jnp.float32)
    return pl.pallas_call(
        kernel,
        out_shape=pltpu.VMEM(queries.shape, queries.dtype),
        in_specs=[hbm] * 3,
        out_specs=pl.BlockSpec(memory_space=pltpu.VMEM),
        scratch_shapes=[
            block, block, block,
            states, state, state, states, states, root, root, root,
            pltpu.VMEM((2, NZ, GROUP * PIECE, DIM), jnp.float32),
            states, state, state, state,
            pltpu.VMEM((DIM, HEADS * DIM), jnp.float32),
            dma((3,)), pltpu.SemaphoreType.REGULAR, pltpu.SemaphoreType.REGULAR,
            dma, dma((2,)), dma, dma((2, N)), dma, dma((2, N)), dma, dma((N,)), dma, dma((N,)),
        ],
        compiler_params=pltpu.CompilerParams(collective_id=0, has_side_effects=True),
        name="prefix_attention",
    )(*(pltpu.with_memory_space_constraint(x, pltpu.HBM) for x in (queries, keys, values)))


def solution(mesh):
    placed = P(("wide", "narrow"), None)
    return jax.shard_map(shards, mesh=mesh, in_specs=(placed,) * 3, out_specs=placed, check_vma=False)
```

```python
import contextlib
import functools

import jax
import jax.numpy as jnp
from jax import lax
from jax.experimental import pallas as pl
from jax.experimental.pallas import tpu as pltpu
from jax.sharding import PartitionSpec as P

HEADS = 16
DIM = 128
GROUP = HEADS // 2
CHUNKS = ((0, 1), (1, 2), (3, 2), (5, 2), (7, 1))
N = len(CHUNKS)
NZ = 8
HALF = NZ // 2
PLANE = 16
PIECE = DIM // PLANE
LAGS = (0, 1, 1, 1, 2, 2, 2, 2)
SIDE = 4
STEPS = sorted(((dx, dy) for dy in range(SIDE) for dx in range(SIDE) if dx or dy),
               key=lambda step: -sum(min(d, SIDE - d) for d in step))
MESH = pl.DeviceIdType.MESH


def scope(name):
    return contextlib.nullcontext()


def dot(a, b, dims):
    return lax.dot_general(a, b, (dims, ((), ())), preferred_element_type=jnp.float32)


def kernel(q_hbm, k_hbm, v_hbm, o_ref, q_ref, k_ref, v_ref, own, part, total, up, prefix, plane, below, pair, zrecv, down,
           carry, give, other, local, in_sem, hello, go,
           ex_send, ex_recv, up_send, up_recv, z_send, z_recv, dn_send, dn_recv, fx_send, fx_recv):
    wide, core = lax.axis_index("wide"), lax.axis_index("narrow")
    here = wide % PLANE
    z = wide // PLANE
    x, y = here % SIDE, here // SIDE
    others = [(y + dy) % SIDE * SIDE + (x + dx) % SIDE for dx, dy in STEPS]
    partner = (wide, 1 - core)
    z_first = jnp.where(z < HALF, 0, 1)
    z_last = jnp.where(z < 2, HALF, NZ)

    def chip_in_plane(i):
        return z * PLANE + i

    def remote(src, dst, send, recv, to):
        return pltpu.make_async_remote_copy(src, dst, send, recv, device_id=to, device_id_type=MESH)

    def arrived(ref, sem):
        pltpu.make_async_copy(ref, ref, sem).wait()

    def rows(k):
        first, count = CHUNKS[k]
        return pl.ds(first * DIM, count * DIM)

    def slice_of(k, i):
        first, count = CHUNKS[k]
        return pl.ds(pl.multiple_of(first * DIM + i * (count * PIECE), 8), count * PIECE)

    def root_rows(k):
        first, count = CHUNKS[k]
        return pl.ds(first * PIECE, count * PIECE)

    def all_but_one(k):
        first, count = CHUNKS[k]
        return pl.ds(first * DIM, (PLANE - 1) * count * PIECE)

    with scope("a_sig"):
        barrier = pltpu.get_barrier_semaphore()
        late = jnp.where(z == 0, x + y > 1, jnp.where(z == 3, x + y > 2, (z < HALF) | ((z == HALF) & (x >= 2) & (y >= 2))))

        @pl.when(jnp.where(late, 1, 0) == core)
        def _():
            pl.semaphore_signal(barrier, inc=1, device_id=partner, device_id_type=MESH)

        for chip in others:
            pl.semaphore_signal(barrier, inc=1, device_id=(chip_in_plane(chip), 0), device_id_type=MESH)

        @pl.when(core == 1)
        def _():
            @pl.loop(z_first, z)
            def _(frm):
                pl.semaphore_signal(barrier, inc=1, device_id=(frm * PLANE + here, 1), device_id_type=MESH)

        loads = [pltpu.make_async_copy(src, dst, in_sem.at[i])
                 for i, (src, dst) in enumerate(((k_hbm, k_ref), (v_hbm, v_ref), (q_hbm, q_ref)))]
        for load in loads:
            load.start()

    z_peers = z_last - 1 - z + jnp.where(z == 1, NZ - HALF, 0)

    def meet_above(count):
        @pl.when(core == 1)
        def _():
            pl.semaphore_wait(barrier, count)
            pl.semaphore_signal(hello, inc=1, device_id=partner, device_id_type=MESH)

        @pl.when(core == 0)
        def _():
            pl.semaphore_wait(hello, 1)

    def meet_plane(count):
        @pl.when(core == 0)
        def _():
            pl.semaphore_wait(barrier, count)
            pl.semaphore_signal(go, inc=1, device_id=partner, device_id_type=MESH)

        @pl.when(core == 1)
        def _():
            pl.semaphore_wait(go, 1)

    def exchange():
        for k in range(N):
            remote(own.at[1 - core, rows(k)], part.at[rows(k)], ex_send, ex_recv.at[min(k, 1)], partner).start()

    def columns(group, head, count=1):
        return pl.ds(pl.multiple_of(group * (GROUP * DIM) + head * DIM, DIM), count * DIM)

    def states(group, k):
        first, count = CHUNKS[k]
        for head in range(first, first + count):
            at = columns(group, head)
            own[group, pl.ds(head * DIM, DIM), :] = dot(k_ref[:, at], v_ref[:, at], ((0,), (0,)))

    with scope("b_load"):
        loads[0].wait()
        loads[1].wait()
    with scope("b_states"):
        for k in range(N):
            states(1 - core, k)
            states(core, k)
    with scope("c_barrier"):
        @pl.when(jnp.logical_not(late))
        def _():
            meet_above(z_peers + 1)
            exchange()
            meet_plane(2 * (PLANE - 1))

        @pl.when(late)
        def _():
            meet_plane(2 * (PLANE - 1) + 1)
            exchange()

    for k in range(N):
        with scope(f"f_exwait{k}"):
            if k < 2:
                rest = GROUP - CHUNKS[k][0] if k else CHUNKS[0][1]
                arrived(part.at[pl.ds(CHUNKS[k][0] * DIM, rest * DIM)], ex_recv.at[k])
        with scope(f"f_up{k}"):
            total[rows(k)] = own[core, rows(k)] + part[rows(k)]
            for root in others:
                remote(total.at[slice_of(k, root)], up.at[core, slice_of(k, here)], up_send, up_recv.at[core, k],
                       (chip_in_plane(root), 1)).start()

            @pl.when(core == 0)
            def _():
                remote(total.at[slice_of(k, here)], up.at[0, slice_of(k, here)], up_send, up_recv.at[0, k], partner).start()

            @pl.when(core == 1)
            def _():
                up[1, slice_of(k, here)] = total[slice_of(k, here)]

    with scope("g_local"):
        loads[2].wait()
        causal = lax.broadcasted_iota(jnp.int32, (DIM, DIM), 0) >= lax.broadcasted_iota(jnp.int32, (DIM, DIM), 1)
        for head in range(HEADS):
            at = pl.ds(head * DIM, DIM)
            scores = dot(q_ref[:, at], k_ref[:, at], ((1,), (1,)))
            scores = jnp.where(causal, scores, 0.0).astype(jnp.bfloat16)
            local[:, at] = dot(scores, v_ref[:, at], ((1,), (0,)))

    with scope("g_meet"):
        @pl.when(late & (core == 1))
        def _():
            pl.semaphore_wait(barrier, z_peers)

    def to_plane(source, g, k, to):
        return remote(source.at[g, root_rows(k)], zrecv.at[g, z, root_rows(k)], z_send, z_recv.at[g, k],
                      (to * PLANE + here, 1))

    def root(g, k):
        with scope(f"h_upwait{k}_{g}"):
            arrived(up.at[g, all_but_one(k) if g else rows(k)], up_recv.at[g, k])
        with scope(f"h_root{k}_{g}"):
            before = jnp.zeros((CHUNKS[k][1] * PIECE, DIM), jnp.float32)
            for i in range(PLANE):
                prefix[g, slice_of(k, i)] = before
                before = before + up[g, slice_of(k, i)]
            plane[g, root_rows(k)] = before

            @pl.loop(0, z_last - 1 - z)
            def _(n):
                to_plane(plane, g, k, z_last - 1 - n).start()

    def earlier(g, k):
        with scope(f"i_zwait{k}_{g}"):
            for n in range(1, NZ - 1):
                @pl.when(z - z_first == n)
                def _():
                    arrived(zrecv.at[g, pl.ds(0, n), root_rows(k)], z_recv.at[g, k])

            below[g, root_rows(k)] = lax.fori_loop(z_first, z, lambda frm, acc: acc + zrecv[g, frm, root_rows(k)],
                                                   jnp.zeros((CHUNKS[k][1] * PIECE, DIM), jnp.float32))

        @pl.when(z == 1)
        def _():
            pair[g, root_rows(k)] = below[g, root_rows(k)] + plane[g, root_rows(k)]
            for to in range(HALF, NZ):
                to_plane(pair, g, k, to).start()

    def carries(g, k):
        with scope(f"i_down{k}_{g}"):
            above = below[g, root_rows(k)]
            for i in range(PLANE):
                down[g, slice_of(k, i)] = prefix[g, slice_of(k, i)] + above
            for late_ones in (False, True):
                for chip in others:
                    @pl.when(((chip % SIDE >= 2) & (chip >= PLANE // 2)) == late_ones)
                    def _():
                        remote(down.at[g, slice_of(k, chip)], carry.at[slice_of(k, here)], dn_send, dn_recv.at[k],
                               (chip_in_plane(chip), g)).start()

            if g:
                carry[slice_of(k, here)] = down[g, slice_of(k, here)]
            else:
                remote(down.at[g, slice_of(k, here)], carry.at[slice_of(k, here)], dn_send, dn_recv.at[k], partner).start()

    @pl.when(core == 1)
    def _():
        for step in range(N + max(LAGS)):
            for g in (1, 0):
                if step < N:
                    root(g, step)
                for lag in sorted(set(LAGS)):
                    if 0 <= step - lag < N:
                        wanted = [i for i in range(NZ) if LAGS[i] == lag]

                        @pl.when(functools.reduce(jnp.logical_or, [z == i for i in wanted]))
                        def _():
                            earlier(g, step - lag)
                            carries(g, step - lag)

    def finish(group, head, state):
        at = columns(group, head)
        high = state.astype(jnp.bfloat16)
        low = (state - high.astype(jnp.float32)).astype(jnp.bfloat16)
        q = q_ref[:, at]
        whole = local[:, at] + (dot(q, high, ((1,), (0,))) + dot(q, low, ((1,), (0,))))
        factor = lax.rsqrt(jnp.mean(whole * whole, axis=-1, keepdims=True) + 1e-05)
        o_ref[:, at] = (whole * factor).astype(jnp.bfloat16)

    def finish_other(k):
        with scope(f"k_fxwait{k}"):
            arrived(other.at[rows(k)], fx_recv.at[k])
        with scope(f"k_fin{k}"):
            first, count = CHUNKS[k]
            for head in range(first, first + count):
                finish(1 - core, head, other[pl.ds(head * DIM, DIM)])

    for k in range(N):
        with scope(f"j_dnwait{k}"):
            @pl.when(core == 0)
            def _():
                arrived(carry.at[rows(k)], dn_recv.at[k])

            @pl.when(core == 1)
            def _():
                arrived(carry.at[all_but_one(k)], dn_recv.at[k])
        with scope(f"j_fin{k}"):
            give[rows(k)] = carry[rows(k)] + jnp.where(core == 0, own[core, rows(k)], 0.0)
            remote(give.at[rows(k)], other.at[rows(k)], fx_send, fx_recv.at[k], partner).start()
            first, count = CHUNKS[k]
            for head in range(first, first + count):
                at = pl.ds(head * DIM, DIM)
                finish(core, head, carry[at] + jnp.where(core == 0, 0.0, part[at]))
        if k:
            finish_other(k - 1)
    finish_other(N - 1)

    with scope("l_waits"):
        arrived(own.at[1 - core], ex_send)
        @pl.when(core == 0)
        def _():
            arrived(total, up_send)

        arrived(give, fx_send)

        @pl.when(core == 1)
        def _():
            most = (PLANE - 1) * GROUP * PIECE
            arrived(total.at[pl.ds(0, most)], up_send)
            arrived(down.reshape(2 * GROUP * DIM, DIM).at[pl.ds(0, GROUP * DIM + most)], dn_send)
            for n in range(1, NZ - 1):
                @pl.when(z_peers == n)
                def _():
                    arrived(zrecv.at[:, pl.ds(0, n)], z_send)


def shards(queries, keys, values):
    dma = pltpu.SemaphoreType.DMA
    hbm = pl.BlockSpec(memory_space=pltpu.HBM)
    block = pltpu.VMEM(queries.shape, queries.dtype)
    state = pltpu.VMEM((GROUP * DIM, DIM), jnp.float32)
    states = pltpu.VMEM((2, GROUP * DIM, DIM), jnp.float32)
    root = pltpu.VMEM((2, GROUP * PIECE, DIM), jnp.float32)
    return pl.pallas_call(
        kernel,
        out_shape=pltpu.VMEM(queries.shape, queries.dtype),
        in_specs=[hbm] * 3,
        out_specs=pl.BlockSpec(memory_space=pltpu.VMEM),
        scratch_shapes=[
            block, block, block,
            states, state, state, states, states, root, root, root,
            pltpu.VMEM((2, NZ, GROUP * PIECE, DIM), jnp.float32),
            states, state, state, state,
            pltpu.VMEM((DIM, HEADS * DIM), jnp.float32),
            dma((3,)), pltpu.SemaphoreType.REGULAR, pltpu.SemaphoreType.REGULAR,
            dma, dma((2,)), dma, dma((2, N)), dma, dma((2, N)), dma, dma((N,)), dma, dma((N,)),
        ],
        compiler_params=pltpu.CompilerParams(collective_id=0, has_side_effects=True),
        name="prefix_attention",
    )(*(pltpu.with_memory_space_constraint(x, pltpu.HBM) for x in (queries, keys, values)))


def solution(mesh):
    placed = P(("wide", "narrow"), None)
    return jax.shard_map(shards, mesh=mesh, in_specs=(placed,) * 3, out_specs=placed, check_vma=False)
```
